256 devices in a mesh: cells: 64 (over z, y, core), tm: 4 (over x).
Axes of the slice: x: 4, y: 4, z: 8, core: 2. Of those that a mesh axis runs over, the one named last changes fastest.
Arguments:
- attitude: float32 [4, 65536], P(None, ('cells', 'tm')), may hold values from -6 to 6
- star_partials: float32 [5, 64, 131072], P(None, None, ('cells', 'tm')), may hold values from -6 to 6
- attitude_partials: float32 [4, 64, 131072], P(None, None, ('cells', 'tm')), may hold values from -6 to 6
- observed: float32 [64, 131072], P(None, ('cells', 'tm')), may hold values from -6 to 6
- phase: float32 [64, 131072], P(None, ('cells', 'tm')), may hold values from 0 to 1
- knot_offset: int32 [64, 131072], P(None, ('cells', 'tm')), may hold values from 0 to 12
- cell_counts: int32 [1024], P(('cells', 'tm')), may hold values from 40 to 64, as said below
- interval_owner: int32 [1024, 64, 1], P(('cells', 'tm')), may hold values from 0 to 255; in each aligned block of 256 rows (0 to 255, 256 to 511, ..., all dimensions but the last counted through in order) at most 2 rows name the same one
- block_slot: int32 [1024, 64], P(('cells', 'tm')), may hold values from 0 to 15
Outputs:
- star_step: float32 [5, 131072], P(None, ('cells', 'tm'))
- attitude_step: float32 [4, 65536], P(None, ('cells', 'tm'))
The draws below stay inside these ranges and needn't reach their ends.
Inputs may be any that keep to these rules, and one draw needn't show every extreme that they name: `interval_owner`: among the 256 transits of the cells of one device no owner is named more than 2 times, and in every draw some owner is named exactly 2 times by the transits of some device. Transits that are not live are listed too. `cell_counts`: some cell has all 64 transits live in every draw.
All inputs are finite; a program needn't handle non-finite values.
Results may differ from the reference program's by a relative error of at most 0.0003.
Values sent between devices are 32-bit elements; how exact they have to be, the bound alone decides.
A program may use at most 128 MiB of HBM per device.

```python
import math
import jax
import jax.numpy as jnp
import numpy as np
from jax import lax

NT = 64
CS = 128
KB = 16
ITERS = 6
BPD = 16
CELLS = 1024
STARS = 131072
TR_DEV = 256
BLOCKS = 4096
KNOTS = 65536
CAP = 2
N_CELLS = 64
N_TM = 4


def draw_cell_counts(key, part):
    first = jax.random.fold_in(key, 11)
    second = jax.random.fold_in(key, 12)
    counts = jax.random.randint(first, (CELLS,), NT * 5 // 8, NT + 1)
    chosen = jax.random.randint(second, (), 0, CELLS)
    return counts.at[chosen].set(NT).astype(jnp.int32)


def with_ends(array, own_key, low, top_value):
    extent = array.shape
    place = [jax.random.randint(jax.random.fold_in(own_key, axis), (), 0, extent[axis]) for axis in range(len(extent))]
    array = array.at[tuple(place)].set(low)
    longest = extent.index(max(extent))
    place[longest] = (place[longest] + 1) % extent[longest]
    return array.at[tuple(place)].set(top_value)


def block_levels(key, dims, cuts, smallest, high):
    loudness, own = 1.0, jax.random.fold_in(key, 6)
    for dim, parts in cuts:
        draws = jnp.exp(jax.random.uniform(jax.random.fold_in(own, dim), (parts,), jnp.float32, smallest / len(cuts), high / len(cuts)))
        loudness = loudness * jnp.repeat(draws, dims[dim] // parts).reshape([-1 if axis == dim else 1 for axis in range(len(dims))])
    return loudness


def routed_block(key, own, number, rows, number_of, top, most, lean):
    sequence = jax.random.permutation(key, number_of)
    crowded, ordinary = portions_of(number_of, rows * top, most, lean, True), portions_of(number_of, rows * top, most, lean, False)
    places = jnp.arange(number_of)

    def named(lengths, offset_by):
        used = int((lengths > 0).sum())
        fixed = max(1, used // 4)
        passed = fixed + (places - fixed + offset_by * (used - fixed)) % max(1, number_of - fixed)
        return jnp.zeros((number_of,), jnp.int32).at[sequence[jnp.where(places < fixed, places, passed)]].set(jnp.asarray(lengths, jnp.int32))

    lengths = jnp.where(number % 4 == 0, named(crowded, number // 4), named(ordinary, number - number // 4 - 1))
    mixed = jax.random.permutation(jax.random.fold_in(own, 3), number_of)
    donor, sink = mixed[0:number_of // 2 * 2:2], mixed[1:number_of // 2 * 2:2]
    room = jnp.minimum(lengths[donor] - 1, most - lengths[sink]) // 2
    room = jnp.where((donor == sequence[0]) | (sink == sequence[0]) | (lengths[sink] == 0), 0, jnp.maximum(room, 0))
    passed = jax.random.randint(jax.random.fold_in(own, 4), (number_of // 2,), 0, 1 << 20) % (room + 1)
    lengths = lengths.at[donor].add(-passed).at[sink].add(passed)
    labels = jnp.searchsorted(jnp.cumsum(lengths), jnp.arange(rows * top), side="right").astype(jnp.int32)
    table = labels.reshape(top, rows).T
    table = table[jax.random.permutation(jax.random.fold_in(own, 1), rows)]
    offset_by = jax.random.randint(jax.random.fold_in(own, 2), (rows, 1), 0, top)
    return jnp.take_along_axis(table, (jnp.arange(top)[None, :] + offset_by) % top, axis=1)


def portions_of(amount, total, bound, lean, full):
    weights = [(1 << 20) // math.isqrt(rank ** lean) + 1 for rank in range(1, amount + 1)]
    largest = bound if full else min(bound, max(-(-total // amount), total * weights[0] // sum(weights)))
    least = 1 if total - largest >= amount - 1 else 0
    given, spare = [largest] + [least] * (amount - 1), total - largest - least * (amount - 1)
    while spare > 0:
        free = [i for i in range(1, amount) if given[i] < largest] or [i for i in range(1, amount) if given[i] < bound]
        mass, budget = sum([weights[i] for i in free]), spare
        for i in free:
            addition = min(bound - given[i], max(1, budget * weights[i] // mass), spare)
            given[i] = given[i] + addition
            spare = spare - addition
    return np.array(given)


def bell_draw(own_key, dims, width, bound, cuts=(), held_as=jnp.bfloat16):
    values = width * jax.random.normal(own_key, dims, jnp.float32)
    if cuts:
        values = values * block_levels(own_key, dims, cuts, -0.22, 0.18)
    return jnp.clip(values, -bound, bound).astype(held_as)


def setup_inputs(seed: int = 0) -> dict:
    streams_of = jax.random.split(jax.random.key(seed), 10)
    attitude = bell_draw(streams_of[0], (4, KNOTS), 1.0, 6.0, ((1, 256),), jnp.float32)
    star_partials = bell_draw(streams_of[1], (5, NT, STARS), 1.0, 6.0, ((2, 256),), jnp.float32)
    attitude_partials = bell_draw(streams_of[2], (4, NT, STARS), 1.0, 6.0, ((2, 256),), jnp.float32)
    observed = bell_draw(streams_of[3], (NT, STARS), 1.0, 6.0, ((1, 256),), jnp.float32)
    phase = jnp.clip(1.0 * jax.random.uniform(streams_of[4], (NT, STARS), jnp.float32) ** block_levels(streams_of[4], (NT, STARS), ((1, 256),), -0.2, 0.2), 0.0, 1.0)
    knot_offset = with_ends(jax.random.randint(streams_of[5], (NT, STARS), 0, KB - 3), jax.random.fold_in(streams_of[5], 1), 0, (KB - 3) - 1).astype(jnp.int32)
    cell_counts = draw_cell_counts(jax.random.fold_in(streams_of[9], 71), 0)
    interval_owner_keys = jax.random.split(jax.random.fold_in(streams_of[7], 1), CELLS * NT // TR_DEV)
    interval_owner_turns = jax.random.permutation(jax.random.fold_in(streams_of[7], 3), CELLS * NT // TR_DEV)
    interval_owner = jax.vmap(lambda own, number: routed_block(jax.random.fold_in(streams_of[7], 2), own, number, TR_DEV, N_CELLS * N_TM, 1, CAP, 2))(interval_owner_keys, interval_owner_turns).reshape((CELLS, NT, 1))
    block_slot = with_ends(jax.random.randint(streams_of[8], (CELLS, NT), 0, BPD), jax.random.fold_in(streams_of[8], 1), 0, BPD - 1).astype(jnp.int32)
    return {"attitude": attitude, "star_partials": star_partials, "attitude_partials": attitude_partials, "observed": observed, "phase": phase, "knot_offset": knot_offset, "cell_counts": cell_counts, "interval_owner": interval_owner, "block_slot": block_slot}


smoothing = 16.0
damping = 2.0
relaxation = 0.5
star_prior = 1.0
highest = lax.Precision.HIGHEST

def spline_basis(phase):
    square = phase * phase
    cube = square * phase
    rest = 1.0 - phase
    return (rest * rest * rest / 6.0, (3.0 * cube - 6.0 * square + 4.0) / 6.0, (-3.0 * cube + 3.0 * square + 3.0 * phase + 1.0) / 6.0, cube / 6.0)

def design_rows(phase, knot_offset, partials, live):
    knots = lax.broadcasted_iota(jnp.int32, (KB, 1), 0)
    basis = spline_basis(phase)
    spread = jnp.zeros(phase.shape[:-1] + (KB, phase.shape[-1]), jnp.float32)
    for order in range(4):
        hit = knots == knot_offset[..., None, :] + order
        spread = spread + jnp.where(hit, basis[order][..., None, :], 0.0)
    spread = spread * live[..., None, None]
    return jnp.moveaxis(partials, 0, -2)[..., :, None, :] * spread[..., None, :, :]

def cholesky_factor(matrix, size):
    lower = [[None for column in range(size)] for row in range(size)]
    for column in range(size):
        total = matrix[column][column]
        for inner in range(column):
            total = total - lower[column][inner] * lower[column][inner]
        pivot = jnp.sqrt(total)
        lower[column][column] = pivot
        for row in range(column + 1, size):
            accum = matrix[row][column]
            for inner in range(column):
                accum = accum - lower[row][inner] * lower[column][inner]
            lower[row][column] = accum / pivot
    return lower

def cholesky_solve(lower, rhs, size):
    forward = []
    for row in range(size):
        accum = rhs[row]
        for inner in range(row):
            accum = accum - lower[row][inner] * forward[inner]
        forward.append(accum / lower[row][row])
    answer = [None for row in range(size)]
    for row in reversed(range(size)):
        accum = forward[row]
        for inner in range(row + 1, size):
            accum = accum - lower[inner][row] * answer[inner]
        answer[row] = accum / lower[row][row]
    return answer

def star_update(partials, first, live):
    normal = [[lax.optimization_barrier(jnp.sum(live * partials[row] * partials[column], axis=0)) + (star_prior if row == column else 0.0) for column in range(5)] for row in range(5)]
    rhs = [lax.optimization_barrier(jnp.sum(partials[row] * first, axis=0)) for row in range(5)]
    lower = cholesky_factor(normal, 5)
    step = cholesky_solve(lower, rhs, 5)
    fitted = partials[0] * step[0]
    for row in range(1, 5):
        fitted = fitted + partials[row] * step[row]
    return (jnp.stack(step), first - live * fitted)

def cell_terms(cell_phase, cell_offset, cell_axis, cell_star, cell_observed, cell_live, cell_values):
    rows = design_rows(cell_phase, cell_offset, cell_axis, cell_live)
    predicted = jnp.einsum('tmas,tma->ts', rows, cell_values, precision=highest)
    first = cell_live[:, None] * cell_observed - predicted
    step, second = star_update(cell_star, first, cell_live[:, None])
    gradient = jnp.einsum('tmas,ts->tma', rows, second, precision=highest)
    return (rows, step, gradient)

def band_products(rows):
    pieces = []
    for shift in range(4):
        left = rows[..., :KB - shift, :]
        right = rows[..., shift:, :]
        product = jnp.einsum('...mas,...nas->...mna', left, right, precision=highest)
        filler = jnp.zeros(product.shape[:-1] + (shift,), jnp.float32)
        pieces.append(jnp.concatenate([product, filler], axis=-1))
    return jnp.stack(pieces, axis=-2)

def band_apply(band, vector):
    result = jnp.einsum('bmna,nba->mba', band[:, :, :, 0, :], vector, precision=highest)
    for shift in range(1, 4):
        filler = jnp.zeros(vector.shape[:-1] + (shift,), jnp.float32)
        ahead = jnp.concatenate([vector[..., shift:], filler], axis=-1)
        result = result + jnp.einsum('bmna,nba->mba', band[:, :, :, shift, :], ahead, precision=highest)
        lagged = jnp.einsum('bnma,nba->mba', band[:, :, :, shift, :], vector, precision=highest)
        result = result + jnp.concatenate([filler, lagged[..., :KB - shift]], axis=-1)
    return result

def diagonal_factor(band):
    shifted = 2.0 * smoothing + damping
    entries = [[band[:, row, column, 0, :] + (shifted if row == column else 0.0) for column in range(4)] for row in range(4)]
    return cholesky_factor(entries, 4)

def sweep(band, lower, gradient, solution, padded):
    count = band.shape[0]
    applied = band_apply(band, solution.reshape(4, count, KB))
    regular = smoothing * (2.0 * solution - padded[:, :-2] - padded[:, 2:]) + damping * solution
    misfit = gradient - applied - regular.reshape(4, count, KB)
    correction = cholesky_solve(lower, [misfit[row] for row in range(4)], 4)
    return solution + relaxation * jnp.stack(correction).reshape(4, count * KB)

def reference(attitude, star_partials, attitude_partials, observed, phase, knot_offset, cell_counts, interval_owner, block_slot):
    block_ids = (interval_owner[:, :, 0] * BPD + block_slot).astype(jnp.int32)
    blocks = attitude.reshape(4, BLOCKS, KB).transpose(1, 0, 2)
    transit = lax.broadcasted_iota(jnp.int32, (CELLS, NT), 1)
    live = jnp.where(transit < cell_counts[:, None], 1.0, 0.0).astype(jnp.float32)
    items = (phase.reshape(NT, CELLS, CS).transpose(1, 0, 2), knot_offset.reshape(NT, CELLS, CS).transpose(1, 0, 2), attitude_partials.reshape(4, NT, CELLS, CS).transpose(2, 0, 1, 3), star_partials.reshape(5, NT, CELLS, CS).transpose(2, 0, 1, 3), observed.reshape(NT, CELLS, CS).transpose(1, 0, 2), live, block_ids)

    def per_cell(carry, pieces):
        band_sum, grad_sum = carry
        cell_phase, cell_offset, cell_axis, cell_star, cell_observed, cell_live, ids = pieces
        rows, step, gradient = cell_terms(cell_phase, cell_offset, cell_axis, cell_star, cell_observed, cell_live, blocks[ids])
        band_sum = band_sum.at[ids].add(band_products(rows))
        grad_sum = grad_sum.at[ids].add(gradient)
        return ((band_sum, grad_sum), step)
    start = (jnp.zeros((BLOCKS, 4, 4, 4, KB), jnp.float32), jnp.zeros((BLOCKS, 4, KB), jnp.float32))
    (band_sum, grad_sum), steps = lax.scan(per_cell, start, items)
    star_step = steps.transpose(1, 0, 2).reshape(5, STARS)
    gradient = grad_sum.transpose(1, 0, 2)
    lower = diagonal_factor(band_sum)
    solution = jnp.zeros((4, KNOTS), jnp.float32)
    for index in range(ITERS):
        padded = jnp.pad(solution, ((0, 0), (1, 1)))
        solution = sweep(band_sum, lower, gradient, solution, padded)
    return (star_step, solution)
```

```python
import functools

import jax
import jax.numpy as jnp
from jax import lax
from jax.experimental import pallas as pl
from jax.experimental.pallas import tpu as pltpu
from jax.sharding import PartitionSpec as P

NT, CS, KB, ITERS = 64, 128, 16, 6
NX, NY, NZ, NC = 4, 4, 8, 2
NP = NX * NY
DEV = NP * NZ * NC
QIN = NZ * NC
CELLS_HERE = 4
TR = CELLS_HERE * NT
ID_LANE = 63
MESH = pl.DeviceIdType.MESH
f32, bf16 = jnp.float32, jnp.bfloat16
PAIRS = [(m, n) for m in range(4) for n in range(m, 4)]
PAIR_OF = {pair: i for i, pair in enumerate(PAIRS)}
PAIR_ROW = [i if i < 5 else i + 3 for i in range(10)]
SHIFTS = [(t, i) for t in range(4) for i in range(4 - t)]
SHIFT_OF = {pair: i for i, pair in enumerate(SHIFTS)}
VMEM = pl.BlockSpec(memory_space=pltpu.VMEM)
SMEM = pl.BlockSpec(memory_space=pltpu.SMEM)


def place():
    cells, x = lax.axis_index("cells"), lax.axis_index("tm")
    z, y, c = cells // (NY * NC), (cells // NC) % NY, cells % NC
    return x, y, z, c


def device(x, y, z, c):
    return ((z * NY + y) * NC + c, x)


def remote(src, dst, send, recv, target):
    return pltpu.make_async_remote_copy(
        src_ref=src, dst_ref=dst, send_sem=send, recv_sem=recv, device_id=target, device_id_type=MESH
    )


def plane_peers(x, y, z, c):
    here = x * NY + y
    peers = []
    for i in range(1, NP):
        there = (here + i) % NP
        peers.append((there, device(there // NY, there % NY, z, c)))
    return peers


def column_peers(x, y, z, c):
    return [((z + i) % NZ, device(x, y, (z + i) % NZ, c)) for i in range(1, NZ)]


def greet(targets):
    barrier = pltpu.get_barrier_semaphore()
    for target in targets:
        pl.semaphore_signal(barrier, inc=1, device_id=target, device_id_type=MESH)
    pl.semaphore_wait(barrier, len(targets))


def gather_kernel(att_ref, out_ref, zs, zr, ps, pr, cs, cr):
    x, y, z, c = place()
    plane, column = plane_peers(x, y, z, c), column_peers(x, y, z, c)
    partner = device(x, y, z, 1 - c)
    greet([t for _, t in plane] + [t for _, t in column] + [partner])
    out_ref[z, y, c, x, 0:4, :] = att_ref[:, 0:128]
    out_ref[z, y, c, x, 4:8, :] = att_ref[:, 128:256]
    mine = out_ref.at[z, y, c, x]
    first = [remote(mine, mine, zs.at[i], zr.at[i], t) for i, (_, t) in enumerate(column)]
    for copy in first:
        copy.start()
    for copy in first:
        copy.wait_recv()
    mine = out_ref.at[:, y, c, x]
    second = [remote(mine, mine, ps.at[i], pr.at[i], t) for i, (_, t) in enumerate(plane)]
    for copy in second:
        copy.start()
    for copy in second:
        copy.wait_recv()
    mine = out_ref.at[:, :, c]
    third = remote(mine, mine, cs, cr, partner)
    third.start()
    for copy in first + second:
        copy.wait_send()
    third.wait()


def split(value):
    high = value.astype(bf16)
    low = (value - high.astype(f32)).astype(bf16)
    return high, low


def cholesky(entries, size):
    lower = [[None] * size for _ in range(size)]
    inverse = [None] * size
    for col in range(size):
        total = entries(col, col)
        for k in range(col):
            total = total - lower[col][k] * lower[col][k]
        inverse[col] = 1.0 / jnp.sqrt(total)
        for row in range(col + 1, size):
            acc = entries(row, col)
            for k in range(col):
                acc = acc - lower[row][k] * lower[col][k]
            lower[row][col] = acc * inverse[col]
    return lower, inverse


def substitute(lower, inverse, rhs, size):
    forward = []
    for row in range(size):
        acc = rhs[row]
        for k in range(row):
            acc = acc - lower[row][k] * forward[k]
        forward.append(acc * inverse[row])
    answer = [None] * size
    for row in reversed(range(size)):
        acc = forward[row]
        for k in range(row + 1, size):
            acc = acc - lower[k][row] * answer[k]
        answer[row] = acc * inverse[row]
    return answer


def crossing_kernel(
    counts, owners, slots, att, star, axis, observed, phase, offset,
    step_ref, pay, basis, cross, pairs, table, first, offs, sums, used, where_to,
):
    def clear(i, carry):
        pay[pl.ds(i * 64, 64), :] = jnp.zeros((64, 128), f32)
        return carry

    lax.fori_loop(0, 11 * DEV // 64, clear, 0)

    def clear_used(i, carry):
        used[i] = 0
        return carry

    lax.fori_loop(0, DEV, clear_used, 0)
    for pad in (5, 6, 7, 13, 14, 15):
        pairs[pad * TR:(pad + 1) * TR, :] = jnp.zeros((TR, 128), f32)
    sub8 = lax.broadcasted_iota(jnp.int32, (8, 128), 0)
    lane8 = lax.broadcasted_iota(jnp.int32, (8, 128), 1)

    for c in range(CELLS_HERE):
        lanes = slice(c * CS, (c + 1) * CS)

        def prepare(g, acc, c=c, lanes=lanes):
            rows = pl.ds(pl.multiple_of(g * 8, 8), 8)
            here = c * NT + g * 8
            live = jnp.where(sub8 + g * 8 < counts[c], 1.0, 0.0)
            t = phase[rows, lanes]
            square = t * t
            cube = square * t
            rest = 1.0 - t
            b = [
                rest * rest * rest * (1.0 / 6.0) * live,
                (3.0 * cube - 6.0 * square + 4.0) * (1.0 / 6.0) * live,
                (-3.0 * cube + 3.0 * square + 3.0 * t + 1.0) * (1.0 / 6.0) * live,
                cube * (1.0 / 6.0) * live,
            ]
            offs[pl.ds(pl.multiple_of(here, 8), 8), :] = offset[rows, lanes]
            for i in range(4):
                basis[pl.ds(pl.multiple_of(i * TR + here, 8), 8), :] = b[i]
            for n, (shift, i) in enumerate(SHIFTS):
                cross[pl.ds(pl.multiple_of(n * TR + here, 8), 8), :] = b[i] * b[i + shift]
            a = [axis[m, rows, lanes] for m in range(4)]
            for n, (i, j) in enumerate(PAIRS):
                pairs[pl.ds(pl.multiple_of(PAIR_ROW[n] * TR + here, 8), 8), :] = a[i] * a[j]
            p = [star[m, rows, lanes] * live for m in range(5)]
            terms = [p[i] * p[j] for i in range(5) for j in range(i + 1)]
            return tuple(s + term for s, term in zip(acc, terms))

        acc = lax.fori_loop(0, NT // 8, prepare, tuple(jnp.zeros((8, 128), f32) for _ in range(15)))
        for n in range(15):
            sums[n:n + 1, lanes] = jnp.sum(acc[n], axis=0, keepdims=True)

    knot = lax.broadcasted_iota(jnp.int32, (16, 128), 0)

    def spread(rows, hits, count):
        value = jnp.zeros((16, 128), f32)
        for i in reversed(range(count)):
            value = jnp.where(hits[i], jnp.broadcast_to(rows[i], (16, 128)), value)
        return value

    def hits_of(at):
        row = offs[pl.ds(at, 1), :]
        gap = knot - jnp.broadcast_to(row, (16, 128))
        return [gap == i for i in range(4)]

    def normals(g, carry):
        c, base = g // 8, (g % 8) * 8
        for jj in range(8):
            j = base + jj
            at = g * 8 + jj
            hits = hits_of(at)
            parts = []
            for shift in range(4):
                rows = [cross[pl.ds(SHIFT_OF[(shift, i)] * TR + at, 1), :] for i in range(4 - shift)]
                parts.append(spread(rows, hits, 4 - shift))
            right = jnp.concatenate(parts, axis=0)
            left = pairs[pl.ds(at, 16, stride=TR), :]
            rh, rl = split(right)
            lh, ll = split(left)
            out = lax.dot_general(
                jnp.concatenate([lh, ll], axis=0), jnp.concatenate([rh, rl], axis=0),
                (((1,), (1,)), ((), ())), preferred_element_type=f32,
            )
            total = out[0:16] + out[16:32]
            total = total + pltpu.roll(total, 64, 1)
            packed = jnp.where(lane8 < 64, total[0:8], total[8:16])
            owner, slot = owners[c, j], slots[c, j]
            rank = used[owner]
            used[owner] = rank + 1
            ox, oc, oy, oz = owner % 4, (owner // 4) % 2, (owner // 8) % 4, owner // 32
            q = (ox * NY + oy) * QIN + oc * NZ + oz
            where_to[at] = q + rank * DEV
            packed = jnp.where((sub8 == 0) & (lane8 == ID_LANE), slot.astype(f32), packed)
            pay[pl.ds(rank * 5 * DEV + q, 5, stride=DEV), :] = packed[0:5]
            rows4 = att[pl.ds(owner * 8 + (slot // 8) * 4, 4), :]
            table[pl.ds(at, 4, stride=TR), :] = pltpu.roll(rows4, (128 - (slot % 8) * 16) % 128, 1)
        return carry

    lax.fori_loop(0, TR // 8, normals, 0)

    for c in range(CELLS_HERE):
        lanes = slice(c * CS, (c + 1) * CS)

        def predict(g, acc, c=c, lanes=lanes):
            rows = pl.ds(pl.multiple_of(g * 8, 8), 8)
            here = c * NT + g * 8
            live = jnp.where(sub8 + g * 8 < counts[c], 1.0, 0.0)
            off = offset[rows, lanes]
            value = live * observed[rows, lanes]
            b = [basis[pl.ds(pl.multiple_of(i * TR + here, 8), 8), :] for i in range(4)]
            for m in range(4):
                tab = table[pl.ds(pl.multiple_of(m * TR + here, 8), 8), :]
                fit = b[0] * jnp.take_along_axis(tab, off, axis=1)
                for i in range(1, 4):
                    fit = fit + b[i] * jnp.take_along_axis(tab, off + i, axis=1)
                value = value - axis[m, rows, lanes] * fit
            first[pl.ds(pl.multiple_of(here, 8), 8), :] = value
            return tuple(s + star[n, rows, lanes] * value for n, s in enumerate(acc))

        acc = lax.fori_loop(0, NT // 8, predict, tuple(jnp.zeros((8, 128), f32) for _ in range(5)))
        for n in range(5):
            sums[15 + n:16 + n, lanes] = jnp.sum(acc[n], axis=0, keepdims=True)

    def entry(i, j):
        n = i * (i + 1) // 2 + j
        return sums[n:n + 1, :] + (1.0 if i == j else 0.0)

    lower, inverse = cholesky(entry, 5)
    steps = substitute(lower, inverse, [sums[15 + n:16 + n, :] for n in range(5)], 5)
    for n in range(5):
        step_ref[n:n + 1, :] = steps[n]

    lane32 = lax.broadcasted_iota(jnp.int32, (32, 128), 1)
    row32 = lax.broadcasted_iota(jnp.int32, (32, 128), 0)
    own = (lane32 // 16) == (row32 % 8)
    lane1 = lax.broadcasted_iota(jnp.int32, (1, 128), 1)

    def gradients(g, carry):
        c, base = g // 8, pl.multiple_of((g % 8) * 8, 8)
        rows = pl.ds(base, 8)
        lanes = pl.ds(pl.multiple_of(c * CS, CS), CS)
        at = pl.multiple_of(g * 8, 8)
        live = jnp.where(sub8 + base < counts[c], 1.0, 0.0)
        fitted = star[0, rows, lanes] * step_ref[0:1, lanes]
        for n in range(1, 5):
            fitted = fitted + star[n, rows, lanes] * step_ref[n:n + 1, lanes]
        second = first[pl.ds(at, 8), :] - live * fitted
        left = jnp.concatenate([axis[m, rows, lanes] * second for m in range(4)], axis=0)
        parts = []
        for jj in range(8):
            hits = hits_of(at + jj)
            parts.append(spread([basis[pl.ds(i * TR + at + jj, 1), :] for i in range(4)], hits, 4))
        lh, ll = split(left)
        rh, rl = split(jnp.concatenate(parts, axis=0))
        out = lax.dot_general(
            jnp.concatenate([lh, ll], axis=0), jnp.concatenate([rh, rl], axis=0),
            (((1,), (1,)), ((), ())), preferred_element_type=f32,
        )
        total = out[0:32, 0:128] + out[0:32, 128:256] + out[32:64, 0:128]
        total = jnp.where(own, total, 0.0)
        for shift in (64, 32, 16):
            total = total + pltpu.roll(total, shift, 1)
        grad = jnp.zeros((8, 128), f32)
        for m in range(4):
            grad = jnp.where((lane8 // 16) % 4 == m, total[m * 8:(m + 1) * 8], grad)
        for jj in range(8):
            code = where_to[at + jj]
            q, rank = code % DEV, code // DEV
            old = pay[pl.ds(10 * DEV + q, 1), :]
            pay[pl.ds(10 * DEV + q, 1), :] = jnp.where(lane1 // 64 == rank, grad[jj:jj + 1], old)
        return carry

    lax.fori_loop(0, TR // 8, gradients, 0)


def exchange_kernel(pay, out, got, comb, part, zsum, zgot, ps, pr, cs, cr, zs, zr, hs, hr):
    x, y, z, c = place()
    plane, column = plane_peers(x, y, z, c), column_peers(x, y, z, c)
    partner = device(x, y, z, 1 - c)
    rank = ((z * NY + y) * NC + c) * NX + x
    after, before = (rank + 1) % DEV, (rank + DEV - 1) % DEV
    right, left = (after // NX, after % NX), (before // NX, before % NX)
    greet([t for _, t in plane] + [t for _, t in column] + [partner, right, left])
    here = x * NY + y
    copies = [
        remote(pay.at[:, pl.ds(p * QIN, QIN), :], got.at[here], ps.at[i], pr.at[i], t)
        for i, (p, t) in enumerate(plane)
    ]
    for copy in copies:
        copy.start()
    got[here] = pay[:, pl.ds(pl.multiple_of(here * QIN, QIN), QIN), :]
    for copy in copies:
        copy.wait_recv()

    rows = NP * QIN
    cols = QIN * KB
    row = lax.broadcasted_iota(jnp.int32, (rows, cols), 0)
    col = lax.broadcasted_iota(jnp.int32, (rows, cols), 1)
    local = (col - (row % QIN) * KB).astype(f32)
    picks = []
    for s in range(2):
        ids = got[:, s * 5, :, :].reshape(rows, 128)[:, ID_LANE:ID_LANE + 1]
        picks.append(jnp.where(local == ids, 1.0, 0.0).T)
    pick = jnp.concatenate(picks, axis=1).astype(bf16)
    lane = lax.broadcasted_iota(jnp.int32, (rows, 128), 1)
    for r in range(6):
        if r < 5:
            data = jnp.concatenate([got[:, s * 5 + r, :, :].reshape(rows, 128) for s in range(2)], axis=0)
        else:
            both = got[:, 10, :, :].reshape(rows, 128)
            data = jnp.concatenate([jnp.where(lane < 64, both, 0.0), jnp.where(lane < 64, 0.0, both)], axis=0)
        high, low = split(data)
        comb[r] = jnp.dot(pick, high, preferred_element_type=f32) + jnp.dot(pick, low, preferred_element_type=f32)

    half = NZ * KB
    swap = remote(comb.at[:, pl.ds(pl.multiple_of((1 - c) * half, half), half), :], part, cs, cr, partner)
    swap.start()
    swap.wait_recv()
    zsum[...] = comb[:, pl.ds(pl.multiple_of(c * half, half), half), :] + part[...]
    along = [
        remote(zsum.at[:, pl.ds(zz * KB, KB), :], zgot.at[z], zs.at[i], zr.at[i], t)
        for i, (zz, t) in enumerate(column)
    ]
    for copy in along:
        copy.start()
    zgot[z] = zsum[:, pl.ds(pl.multiple_of(z * KB, KB), KB), :]
    for copy in along:
        copy.wait_recv()
    total = zgot[0]
    for i in range(1, NZ):
        total = total + zgot[i]
    out[:, 8:24, :] = total
    halo = [
        remote(out.at[:, 16:24, :], out.at[:, 0:8, :], hs.at[0], hr.at[0], right),
        remote(out.at[:, 8:16, :], out.at[:, 24:32, :], hs.at[1], hr.at[1], left),
    ]
    for copy in halo:
        copy.start()
    for copy in copies + [swap] + along:
        copy.wait_send()
    for copy in halo:
        copy.wait()


def sweep_kernel(red, out):
    rank = lax.axis_index("cells") * NX + lax.axis_index("tm")
    shape = (32, 128)
    row = lax.broadcasted_iota(jnp.int32, shape, 0)
    lane = lax.broadcasted_iota(jnp.int32, shape, 1)
    k = lane % KB
    beyond = ((row == 7) & (rank == 0)) | ((row == 24) & (rank == DEV - 1))
    valid = jnp.where(beyond, 0.0, 1.0)
    ahead, behind = {}, {}
    for n in range(10):
        comp = red[n % 5]
        start = (n // 5) * 64
        for t in range(4):
            value = jnp.take_along_axis(comp, start + t * 16 + k, axis=1)
            ahead[n, t] = jnp.where(k + t < KB, value, 0.0) if t else value
            if t:
                value = jnp.take_along_axis(comp, start + t * 16 + (k + KB - t) % KB, axis=1)
                behind[n, t] = jnp.where(k >= t, value, 0.0)
    for n, (i, j) in enumerate(PAIRS):
        if i == j:
            ahead[n, 0] = ahead[n, 0] + 34.0
    fold = red[5]
    fold = fold + pltpu.roll(fold, 64, 1)
    gradient = [jnp.take_along_axis(fold, m * KB + k, axis=1) for m in range(4)]

    def pair(i, j):
        return PAIR_OF[(min(i, j), max(i, j))]

    lower, inverse = cholesky(lambda i, j: ahead[pair(i, j), 0], 4)
    x = [0.5 * v * valid for v in substitute(lower, inverse, gradient, 4)]
    for _ in range(ITERS - 1):
        misfit = list(gradient)
        for n in range(4):
            up = {t: pltpu.roll(x[n], 128 - t, 1) for t in (1, 2, 3)}
            down = {t: pltpu.roll(x[n], t, 1) for t in (1, 2, 3)}
            for m in range(4):
                p = pair(m, n)
                acc = ahead[p, 0] * x[n]
                for t in (1, 2, 3):
                    acc = acc + ahead[p, t] * up[t] + behind[p, t] * down[t]
                misfit[m] = misfit[m] - acc
            before = jnp.where(k == 0, pltpu.roll(down[1], 1, 0), down[1])
            after = jnp.where(k == KB - 1, pltpu.roll(up[1], 31, 0), up[1])
            misfit[n] = misfit[n] + 16.0 * (before + after)
        x = [(v + 0.5 * w) * valid for v, w in zip(x, substitute(lower, inverse, misfit, 4))]
    sub8 = lax.broadcasted_iota(jnp.int32, (8, 128), 0)
    keep = sub8 == lax.broadcasted_iota(jnp.int32, (8, 128), 1) // KB
    for m in range(4):
        for h in range(2):
            part = jnp.where(keep, x[m][8 + h * 8:16 + h * 8], 0.0)
            out[m:m + 1, h * 128:(h + 1) * 128] = jnp.sum(part, axis=0, keepdims=True)


def per_device(
    attitude, star_partials, attitude_partials, observed, phase, knot_offset, cell_counts, interval_owner, block_slot
):
    dma = pltpu.SemaphoreType.DMA
    whole = pl.pallas_call(
        gather_kernel,
        out_shape=jax.ShapeDtypeStruct((NZ, NY, NC, NX, 8, 128), f32),
        in_specs=[VMEM],
        out_specs=VMEM,
        scratch_shapes=[dma((NZ - 1,)), dma((NZ - 1,)), dma((NP - 1,)), dma((NP - 1,)), dma, dma],
        compiler_params=pltpu.CompilerParams(collective_id=0, has_side_effects=True),
        name="gather_attitude",
    )(attitude)
    star_step, pay = pl.pallas_call(
        crossing_kernel,
        out_shape=(
            jax.ShapeDtypeStruct((5, CELLS_HERE * CS), f32),
            jax.ShapeDtypeStruct((11 * DEV, 128), f32),
        ),
        in_specs=[SMEM, SMEM, SMEM] + [VMEM] * 6,
        out_specs=(VMEM, VMEM),
        scratch_shapes=[
            pltpu.VMEM((4 * TR, 128), f32),
            pltpu.VMEM((10 * TR, 128), f32),
            pltpu.VMEM((16 * TR, 128), f32),
            pltpu.VMEM((4 * TR, 128), f32),
            pltpu.VMEM((TR, 128), f32),
            pltpu.VMEM((TR, 128), jnp.int32),
            pltpu.VMEM((24, CELLS_HERE * CS), f32),
            pltpu.SMEM((DEV,), jnp.int32),
            pltpu.SMEM((TR,), jnp.int32),
        ],
        name="crossings",
    )(
        cell_counts, interval_owner.reshape(CELLS_HERE, NT), block_slot, whole.reshape(DEV * 8, 128),
        star_partials, attitude_partials, observed, phase, knot_offset,
    )
    reduced = pl.pallas_call(
        exchange_kernel,
        out_shape=jax.ShapeDtypeStruct((6, 32, 128), f32),
        in_specs=[VMEM],
        out_specs=VMEM,
        scratch_shapes=[
            pltpu.VMEM((NP, 11, QIN, 128), f32),
            pltpu.VMEM((6, QIN * KB, 128), f32),
            pltpu.VMEM((6, NZ * KB, 128), f32),
            pltpu.VMEM((6, NZ * KB, 128), f32),
            pltpu.VMEM((NZ, 6, KB, 128), f32),
            dma((NP - 1,)), dma((NP - 1,)), dma, dma, dma((NZ - 1,)), dma((NZ - 1,)), dma((2,)), dma((2,)),
        ],
        compiler_params=pltpu.CompilerParams(collective_id=1, has_side_effects=True),
        name="exchange",
    )(pay.reshape(11, DEV, 128))
    attitude_step = pl.pallas_call(
        sweep_kernel,
        out_shape=jax.ShapeDtypeStruct((4, 256), f32),
        in_specs=[VMEM],
        out_specs=VMEM,
        name="sweeps",
    )(reduced)
    return (star_step, attitude_step)


def solution(mesh):
    both = ("cells", "tm")
    placed = (
        P(None, both), P(None, None, both), P(None, None, both), P(None, both), P(None, both), P(None, both),
        P(both), P(both, None, None), P(both, None),
    )
    return jax.shard_map(
        per_device, mesh=mesh, in_specs=placed, out_specs=(P(None, both), P(None, both)), check_vma=False
    )
```

```python
import functools

import jax
import jax.numpy as jnp
from jax import lax
from jax.experimental import pallas as pl
from jax.experimental.pallas import tpu as pltpu
from jax.sharding import PartitionSpec as P

NT, CS, KB, ITERS = 64, 128, 16, 6
NX, NY, NZ, NC = 4, 4, 8, 2
NP = NX * NY
DEV = NP * NZ * NC
QIN = NZ * NC
CELLS_HERE = 4
TR = CELLS_HERE * NT
ID_LANE = 63
MESH = pl.DeviceIdType.MESH
f32, bf16 = jnp.float32, jnp.bfloat16
PAIRS = [(m, n) for m in range(4) for n in range(m, 4)]
PAIR_OF = {pair: i for i, pair in enumerate(PAIRS)}
SHIFTS = [(t, i) for t in range(4) for i in range(4 - t)]
SHIFT_OF = {pair: i for i, pair in enumerate(SHIFTS)}
VMEM = pl.BlockSpec(memory_space=pltpu.VMEM)
SMEM = pl.BlockSpec(memory_space=pltpu.SMEM)


def place():
    cells, x = lax.axis_index("cells"), lax.axis_index("tm")
    z, y, c = cells // (NY * NC), (cells // NC) % NY, cells % NC
    return x, y, z, c


def device(x, y, z, c):
    return ((z * NY + y) * NC + c, x)


def remote(src, dst, send, recv, target):
    return pltpu.make_async_remote_copy(
        src_ref=src, dst_ref=dst, send_sem=send, recv_sem=recv, device_id=target, device_id_type=MESH
    )


def plane_peers(x, y, z, c):
    here = x * NY + y
    peers = []
    for i in range(1, NP):
        there = (here + i) % NP
        peers.append((there, device(there // NY, there % NY, z, c)))
    return peers


def column_peers(x, y, z, c):
    return [((z + i) % NZ, device(x, y, (z + i) % NZ, c)) for i in range(1, NZ)]


def greet(targets):
    barrier = pltpu.get_barrier_semaphore()
    for target in targets:
        pl.semaphore_signal(barrier, inc=1, device_id=target, device_id_type=MESH)
    pl.semaphore_wait(barrier, len(targets))


def split(value):
    high = value.astype(bf16)
    low = (value - high.astype(f32)).astype(bf16)
    return high, low


def cholesky(entries, size):
    lower = [[None] * size for _ in range(size)]
    inverse = [None] * size
    for col in range(size):
        total = entries(col, col)
        for k in range(col):
            total = total - lower[col][k] * lower[col][k]
        inverse[col] = 1.0 / jnp.sqrt(total)
        for row in range(col + 1, size):
            acc = entries(row, col)
            for k in range(col):
                acc = acc - lower[row][k] * lower[col][k]
            lower[row][col] = acc * inverse[col]
    return lower, inverse


def substitute(lower, inverse, rhs, size):
    forward = []
    for row in range(size):
        acc = rhs[row]
        for k in range(row):
            acc = acc - lower[row][k] * forward[k]
        forward.append(acc * inverse[row])
    answer = [None] * size
    for row in reversed(range(size)):
        acc = forward[row]
        for k in range(row + 1, size):
            acc = acc - lower[k][row] * answer[k]
        answer[row] = acc * inverse[row]
    return answer


def spline(t, live):
    square = t * t
    cube = square * t
    rest = 1.0 - t
    return [
        rest * rest * rest * (1.0 / 6.0) * live,
        (3.0 * cube - 6.0 * square + 4.0) * (1.0 / 6.0) * live,
        (-3.0 * cube + 3.0 * square + 3.0 * t + 1.0) * (1.0 / 6.0) * live,
        cube * (1.0 / 6.0) * live,
    ]


def spread(rows, hits):
    value = jnp.zeros((16, 128), f32)
    for row, hit in reversed(list(zip(rows, hits))):
        value = jnp.where(hit, jnp.broadcast_to(row, (16, 128)), value)
    return value


def nt_dot(left, right):
    return lax.dot_general(left, right, (((1,), (1,)), ((), ())), preferred_element_type=f32)


def aligned(value):
    return pl.multiple_of(value, 8)


def normal_kernel(counts, owners, slots, axis, phase, offset, pay, codes, cross, parts, offs, used):
    sub8 = lax.broadcasted_iota(jnp.int32, (8, 128), 0)
    lane8 = lax.broadcasted_iota(jnp.int32, (8, 128), 1)

    def clear(i, carry):
        pay[pl.ds(aligned(i * 128), 128), :] = jnp.zeros((128, 128), f32)
        return carry

    lax.fori_loop(0, 10 * DEV // 128, clear, 0)
    for c in range(CELLS_HERE):
        lanes = slice(c * CS, (c + 1) * CS)

        def prepare(g, carry, c=c, lanes=lanes):
            rows = pl.ds(aligned(g * 8), 8)
            here = c * NT + g * 8
            live = jnp.where(sub8 + g * 8 < counts[c], 1.0, 0.0)
            b = spline(phase[rows, lanes], live)
            offs[pl.ds(aligned(here), 8), :] = offset[rows, lanes]
            for n, (shift, i) in enumerate(SHIFTS):
                cross[pl.ds(aligned(n * TR + here), 8), :] = b[i] * b[i + shift]
            for m in range(4):
                parts[pl.ds(aligned(m * TR + here), 8), :] = axis[m, rows, lanes]
            for i in range(8):
                used[here + i] = 0
            return carry

        lax.fori_loop(0, NT // 8, prepare, 0)

    knot = lax.broadcasted_iota(jnp.int32, (16, 128), 0)

    def normals(g, carry):
        c, base = lax.shift_right_logical(g, 3), (g & 7) * 8
        for jj in range(8):
            at = g * 8 + jj
            gap = knot - jnp.broadcast_to(offs[pl.ds(at, 1), :], (16, 128))
            hits = [gap == i for i in range(4)]
            right = jnp.concatenate(
                [
                    spread([cross[pl.ds(SHIFT_OF[(s, i)] * TR + at, 1), :] for i in range(4 - s)], hits)
                    for s in range(4)
                ],
                axis=0,
            )
            a = [jnp.broadcast_to(parts[pl.ds(m * TR + at, 1), :], (8, 128)) for m in range(4)]
            top = jnp.where(sub8 == 4, a[1], a[0]) * jnp.where(
                sub8 == 0, a[0], jnp.where(sub8 == 2, a[2], jnp.where(sub8 == 3, a[3], a[1]))
            )
            bottom = jnp.where(sub8 < 2, a[1], jnp.where(sub8 == 4, a[3], a[2])) * jnp.where(
                (sub8 == 0) | (sub8 == 2), a[2], a[3]
            )
            rh, rl = split(right)
            lh, ll = split(jnp.concatenate([top, bottom], axis=0))
            out = nt_dot(jnp.concatenate([lh, ll], axis=0), jnp.concatenate([rh, rl], axis=0))
            total = out[0:16] + out[16:32]
            total = total + pltpu.roll(total, 64, 1)
            packed = jnp.where(lane8 < 64, total[0:8], total[8:16])
            owner, slot = owners[c, base + jj], slots[c, base + jj]
            rank = used[owner]
            used[owner] = rank + 1
            plane = ((owner & 3) << 2) | ((owner >> 3) & 3)
            q = (plane << 4) | ((owner & 4) << 1) | (owner >> 5)
            packed = jnp.where((sub8 == 0) & (lane8 == ID_LANE), slot.astype(f32), packed)
            pay[pl.ds(rank * (5 * DEV) + q, 5, stride=DEV), :] = packed[0:5]
            codes[pl.ds(at, 1), :] = jnp.full((1, 128), rank * DEV + q, jnp.int32)
        return carry

    lax.fori_loop(0, TR // 8, normals, 0)


def main_kernel(
    counts, owners, slots, att_in, pay, codes, star, axis, observed, phase, offset,
    step_ref, out,
    att, sh, sl, tile, otile, table, first, sums, order, grads, gpay, got, ggot, comb, part, zsum, zgot,
    zs, zr, ps, pr, cs, cr, ns, nr, gs, gr, ws, wr, us, ur, vs, vr, hs, hr,
):
    x, y, z, c = place()
    plane, column = plane_peers(x, y, z, c), column_peers(x, y, z, c)
    partner = device(x, y, z, 1 - c)
    rank = ((z * NY + y) * NC + c) * NX + x
    after, before = (rank + 1) % DEV, (rank + DEV - 1) % DEV
    right, left = (after // NX, after % NX), (before // NX, before % NX)
    greet([t for _, t in plane] + [t for _, t in column] + [partner, right, left])
    here = x * NY + y
    sent = []

    att[z, y, c, x, 0:4, :] = att_in[:, 0:128]
    att[z, y, c, x, 4:8, :] = att_in[:, 128:256]
    mine = att.at[z, y, c, x]
    gather_z = [remote(mine, mine, zs.at[i], zr.at[i], t) for i, (_, t) in enumerate(column)]
    for copy in gather_z:
        copy.start()

    sub8 = lax.broadcasted_iota(jnp.int32, (8, 128), 0)
    lane8 = lax.broadcasted_iota(jnp.int32, (8, 128), 1)
    knot = lax.broadcasted_iota(jnp.int32, (16, 128), 0)

    def spreads(cell):
        lanes = slice(cell * CS, (cell + 1) * CS)

        def body(g, acc):
            rows = pl.ds(aligned(g * 8), 8)
            live = jnp.where(sub8 + g * 8 < counts[cell], 1.0, 0.0)
            b = spline(phase[rows, lanes], live)
            otile[...] = offset[rows, lanes]
            for i in range(4):
                tile[i * 8:(i + 1) * 8, :] = b[i]
            pieces = []
            for jj in range(8):
                gap = knot - jnp.broadcast_to(otile[jj:jj + 1, :], (16, 128))
                pieces.append(spread([tile[i * 8 + jj:i * 8 + jj + 1, :] for i in range(4)], [gap == i for i in range(4)]))
            high, low = split(jnp.concatenate(pieces, axis=0))
            where = pl.ds(pl.multiple_of((cell * 8 + g) * 128, 128), 128)
            sh[where, :] = high
            sl[where, :] = low
            p = [star[m, rows, lanes] * live for m in range(5)]
            terms = [p[i] * p[j] for i in range(5) for j in range(i + 1)]
            return tuple(s + term for s, term in zip(acc, terms))

        acc = lax.fori_loop(0, NT // 8, body, tuple(jnp.zeros((8, 128), f32) for _ in range(15)))
        for n in range(15):
            sums[n:n + 1, lanes] = jnp.sum(acc[n], axis=0, keepdims=True)

    spreads(0)
    spreads(1)

    for copy in gather_z:
        copy.wait_recv()
    mine = att.at[:, y, c, x]
    gather_p = [remote(mine, mine, ps.at[i], pr.at[i], t) for i, (_, t) in enumerate(plane)]
    for copy in gather_p:
        copy.start()
    terms = [
        remote(pay.at[:, pl.ds(p * QIN, QIN), :], got.at[here], ns.at[i], nr.at[i], t)
        for i, (p, t) in enumerate(plane)
    ]
    for copy in terms:
        copy.start()
    got[here] = pay[:, pl.ds(pl.multiple_of(here * QIN, QIN), QIN), :]

    spreads(2)
    spreads(3)

    def entry(i, j):
        n = i * (i + 1) // 2 + j
        return sums[n:n + 1, :] + (1.0 if i == j else 0.0)

    lower, inverse = cholesky(entry, 5)
    target = lax.broadcasted_iota(jnp.int32, (TR, DEV), 1)
    code = jnp.broadcast_to(codes[:, 0:1], (TR, DEV))
    for s in range(2):
        order[:, s * TR:(s + 1) * TR] = jnp.where(code == target + s * DEV, 1.0, 0.0).T.astype(bf16)

    for copy in gather_p:
        copy.wait_recv()
    mine = att.at[:, :, c]
    gather_c = remote(mine, mine, cs, cr, partner)
    gather_c.start()
    gather_c.wait_recv()

    lane4 = lax.broadcasted_iota(jnp.int32, (4, 128), 1) // KB

    def choose(g, carry):
        cell, base = lax.shift_right_logical(g, 3), (g & 7) * 8
        for jj in range(8):
            owner, slot = owners[cell, base + jj], slots[cell, base + jj]
            rows4 = att[owner >> 5, (owner >> 3) & 3, (owner >> 2) & 1, owner & 3, pl.ds((slot >> 3) * 4, 4), :]
            table[pl.ds(g * 32 + jj, 4, stride=8), :] = jnp.where(lane4 == (slot & 7), rows4, 0.0)
        return carry

    lax.fori_loop(0, TR // 8, choose, 0)

    lane32 = lax.broadcasted_iota(jnp.int32, (32, 128), 1)
    row32 = lax.broadcasted_iota(jnp.int32, (32, 128), 0)
    own = (lane32 // KB) == (row32 % 8)

    def fold(value):
        for shift in (64, 32, 16):
            value = value + pltpu.roll(value, shift, 1)
        return value

    for cell in range(CELLS_HERE):
        lanes = slice(cell * CS, (cell + 1) * CS)

        def predict(g, acc, cell=cell, lanes=lanes):
            rows = pl.ds(aligned(g * 8), 8)
            gg = cell * 8 + g
            live = jnp.where(sub8 + g * 8 < counts[cell], 1.0, 0.0)
            coeff = jnp.where(own, fold(table[pl.ds(aligned(gg * 32), 32), :]), 0.0)
            high, low = split(coeff)
            where = pl.ds(pl.multiple_of(gg * 128, 128), 128)
            big = jnp.dot(jnp.concatenate([high, low], axis=0), sh[where, :], preferred_element_type=f32)
            fit = big[0:32] + big[32:64] + jnp.dot(high, sl[where, :], preferred_element_type=f32)
            value = live * observed[rows, lanes]
            for m in range(4):
                value = value - axis[m, rows, lanes] * fit[m * 8:(m + 1) * 8]
            first[pl.ds(aligned(gg * 8), 8), :] = value
            return tuple(s + star[n, rows, lanes] * value for n, s in enumerate(acc))

        acc = lax.fori_loop(0, NT // 8, predict, tuple(jnp.zeros((8, 128), f32) for _ in range(5)))
        for n in range(5):
            sums[15 + n:16 + n, lanes] = jnp.sum(acc[n], axis=0, keepdims=True)

    steps = substitute(lower, inverse, [sums[15 + n:16 + n, :] for n in range(5)], 5)
    for n in range(5):
        step_ref[n:n + 1, :] = steps[n]

    for cell in range(CELLS_HERE):
        lanes = slice(cell * CS, (cell + 1) * CS)

        def gradients(g, carry, cell=cell, lanes=lanes):
            rows = pl.ds(aligned(g * 8), 8)
            gg = cell * 8 + g
            live = jnp.where(sub8 + g * 8 < counts[cell], 1.0, 0.0)
            fitted = star[0, rows, lanes] * step_ref[0:1, lanes]
            for n in range(1, 5):
                fitted = fitted + star[n, rows, lanes] * step_ref[n:n + 1, lanes]
            second = first[pl.ds(aligned(gg * 8), 8), :] - live * fitted
            high, low = split(jnp.concatenate([axis[m, rows, lanes] * second for m in range(4)], axis=0))
            where = pl.ds(pl.multiple_of(gg * 128, 128), 128)
            big = nt_dot(jnp.concatenate([high, low], axis=0), sh[where, :])
            total = big[0:32] + big[32:64] + nt_dot(high, sl[where, :])
            total = fold(jnp.where(own, total, 0.0))
            grad = jnp.zeros((8, 128), f32)
            for m in range(4):
                grad = jnp.where((lane8 // KB) % 4 == m, total[m * 8:(m + 1) * 8], grad)
            grads[pl.ds(aligned(gg * 8), 8), :] = grad
            return carry

        lax.fori_loop(0, NT // 8, gradients, 0)

    lane = lax.broadcasted_iota(jnp.int32, (TR, 128), 1)

    def halves(both):
        return split(jnp.concatenate([jnp.where(lane < 64, both, 0.0), jnp.where(lane < 64, 0.0, both)], axis=0))

    high, low = halves(grads[...])
    gpay[...] = jnp.dot(order[...], high, preferred_element_type=f32) + jnp.dot(
        order[...], low, preferred_element_type=f32
    )
    gterms = [
        remote(gpay.at[pl.ds(p * QIN, QIN), :], ggot.at[here], gs.at[i], gr.at[i], t) for i, (p, t) in enumerate(plane)
    ]
    for copy in gterms:
        copy.start()
    ggot[here] = gpay[pl.ds(pl.multiple_of(here * QIN, QIN), QIN), :]

    for copy in terms:
        copy.wait_recv()
    rows = NP * QIN
    cols = QIN * KB
    row = lax.broadcasted_iota(jnp.int32, (rows, cols), 0)
    col = lax.broadcasted_iota(jnp.int32, (rows, cols), 1)
    local = (col - (row % QIN) * KB).astype(f32)
    for s in range(2):
        ids = got[:, s * 5, :, :].reshape(rows, 128)[:, ID_LANE:ID_LANE + 1]
        order[:, s * rows:(s + 1) * rows] = jnp.where(local == ids, 1.0, 0.0).T.astype(bf16)
    half = NZ * KB
    keep = pl.ds(pl.multiple_of(c * half, half), half)
    give = pl.ds(pl.multiple_of((1 - c) * half, half), half)

    def combine(r, high, low):
        comb[r] = jnp.dot(order[...], high, preferred_element_type=f32) + jnp.dot(
            order[...], low, preferred_element_type=f32
        )

    for r in range(5):
        data = jnp.concatenate([got[:, s * 5 + r, :, :].reshape(rows, 128) for s in range(2)], axis=0)
        combine(r, *split(data))
    five = pl.ds(0, 5)
    swap = remote(comb.at[five, give, :], part.at[five], ws.at[0], wr.at[0], partner)
    swap.start()
    for copy in gterms:
        copy.wait_recv()
    combine(5, *halves(ggot[...].reshape(rows, 128)))
    gswap = remote(comb.at[5, give, :], part.at[5], ws.at[1], wr.at[1], partner)
    gswap.start()
    swap.wait_recv()
    zsum[0:5] = comb[0:5, keep, :] + part[0:5]
    along = [
        remote(zsum.at[five, pl.ds(zz * KB, KB), :], zgot.at[z, five], us.at[i], ur.at[i], t)
        for i, (zz, t) in enumerate(column)
    ]
    for copy in along:
        copy.start()
    gswap.wait_recv()
    zsum[5] = comb[5, keep, :] + part[5]
    galong = [
        remote(zsum.at[5, pl.ds(zz * KB, KB), :], zgot.at[z, 5], vs.at[i], vr.at[i], t)
        for i, (zz, t) in enumerate(column)
    ]
    for copy in galong:
        copy.start()
    zgot[z] = zsum[:, pl.ds(pl.multiple_of(z * KB, KB), KB), :]
    for copy in along + galong:
        copy.wait_recv()
    total = zgot[0]
    for i in range(1, NZ):
        total = total + zgot[i]
    out[:, 8:24, :] = total
    halo = [
        remote(out.at[:, 16:24, :], out.at[:, 0:8, :], hs.at[0], hr.at[0], right),
        remote(out.at[:, 8:16, :], out.at[:, 24:32, :], hs.at[1], hr.at[1], left),
    ]
    for copy in halo:
        copy.start()
    for copy in gather_z + gather_p + [gather_c] + terms + gterms + [swap, gswap] + along + galong:
        copy.wait_send()
    for copy in halo:
        copy.wait()


def sweep_kernel(red, steps, out, steps_out):
    steps_out[...] = steps[...]
    rank = lax.axis_index("cells") * NX + lax.axis_index("tm")
    shape = (32, 128)
    row = lax.broadcasted_iota(jnp.int32, shape, 0)
    lane = lax.broadcasted_iota(jnp.int32, shape, 1)
    k = lane % KB
    beyond = ((row == 7) & (rank == 0)) | ((row == 24) & (rank == DEV - 1))
    valid = jnp.where(beyond, 0.0, 1.0)
    ahead, behind = {}, {}
    for n in range(10):
        comp = red[n % 5]
        start = (n // 5) * 64
        for t in range(4):
            value = jnp.take_along_axis(comp, start + t * 16 + k, axis=1)
            ahead[n, t] = jnp.where(k + t < KB, value, 0.0) if t else value
            if t:
                value = jnp.take_along_axis(comp, start + t * 16 + (k + KB - t) % KB, axis=1)
                behind[n, t] = jnp.where(k >= t, value, 0.0)
    for n, (i, j) in enumerate(PAIRS):
        if i == j:
            ahead[n, 0] = ahead[n, 0] + 34.0
    fold = red[5]
    fold = fold + pltpu.roll(fold, 64, 1)
    gradient = [jnp.take_along_axis(fold, m * KB + k, axis=1) for m in range(4)]

    def pair(i, j):
        return PAIR_OF[(min(i, j), max(i, j))]

    lower, inverse = cholesky(lambda i, j: ahead[pair(i, j), 0], 4)
    x = [0.5 * v * valid for v in substitute(lower, inverse, gradient, 4)]
    for _ in range(ITERS - 1):
        misfit = list(gradient)
        for n in range(4):
            up = {t: pltpu.roll(x[n], 128 - t, 1) for t in (1, 2, 3)}
            down = {t: pltpu.roll(x[n], t, 1) for t in (1, 2, 3)}
            for m in range(4):
                p = pair(m, n)
                acc = ahead[p, 0] * x[n]
                for t in (1, 2, 3):
                    acc = acc + ahead[p, t] * up[t] + behind[p, t] * down[t]
                misfit[m] = misfit[m] - acc
            before = jnp.where(k == 0, pltpu.roll(down[1], 1, 0), down[1])
            after = jnp.where(k == KB - 1, pltpu.roll(up[1], 31, 0), up[1])
            misfit[n] = misfit[n] + 16.0 * (before + after)
        x = [(v + 0.5 * w) * valid for v, w in zip(x, substitute(lower, inverse, misfit, 4))]
    sub8 = lax.broadcasted_iota(jnp.int32, (8, 128), 0)
    keep = sub8 == lax.broadcasted_iota(jnp.int32, (8, 128), 1) // KB
    for m in range(4):
        for h in range(2):
            part = jnp.where(keep, x[m][8 + h * 8:16 + h * 8], 0.0)
            out[m:m + 1, h * 128:(h + 1) * 128] = jnp.sum(part, axis=0, keepdims=True)


def per_device(
    attitude, star_partials, attitude_partials, observed, phase, knot_offset, cell_counts, interval_owner, block_slot
):
    dma = pltpu.SemaphoreType.DMA
    owners = interval_owner.reshape(CELLS_HERE, NT)
    pay, codes = pl.pallas_call(
        normal_kernel,
        out_shape=(
            jax.ShapeDtypeStruct((10 * DEV, 128), f32),
            jax.ShapeDtypeStruct((TR, 128), jnp.int32),
        ),
        in_specs=[SMEM, SMEM, SMEM] + [VMEM] * 3,
        out_specs=(VMEM, VMEM),
        scratch_shapes=[
            pltpu.VMEM((10 * TR, 128), f32),
            pltpu.VMEM((4 * TR, 128), f32),
            pltpu.VMEM((TR, 128), jnp.int32),
            pltpu.SMEM((DEV,), jnp.int32),
        ],
        name="normal_terms",
    )(cell_counts, owners, block_slot, attitude_partials, phase, knot_offset)
    peers, column = NP - 1, NZ - 1
    steps, reduced = pl.pallas_call(
        main_kernel,
        out_shape=(
            jax.ShapeDtypeStruct((5, CELLS_HERE * CS), f32),
            jax.ShapeDtypeStruct((6, 32, 128), f32),
        ),
        in_specs=[SMEM, SMEM, SMEM] + [VMEM] * 8,
        out_specs=(VMEM, VMEM),
        scratch_shapes=[
            pltpu.VMEM((NZ, NY, NC, NX, 8, 128), f32),
            pltpu.VMEM((TR * KB, 128), bf16),
            pltpu.VMEM((TR * KB, 128), bf16),
            pltpu.VMEM((32, 128), f32),
            pltpu.VMEM((8, 128), jnp.int32),
            pltpu.VMEM((4 * TR, 128), f32),
            pltpu.VMEM((TR, 128), f32),
            pltpu.VMEM((24, CELLS_HERE * CS), f32),
            pltpu.VMEM((DEV, 2 * TR), bf16),
            pltpu.VMEM((TR, 128), f32),
            pltpu.VMEM((DEV, 128), f32),
            pltpu.VMEM((NP, 10, QIN, 128), f32),
            pltpu.VMEM((NP, QIN, 128), f32),
            pltpu.VMEM((6, QIN * KB, 128), f32),
            pltpu.VMEM((6, NZ * KB, 128), f32),
            pltpu.VMEM((6, NZ * KB, 128), f32),
            pltpu.VMEM((NZ, 6, KB, 128), f32),
            dma((column,)), dma((column,)), dma((peers,)), dma((peers,)), dma, dma,
            dma((peers,)), dma((peers,)), dma((peers,)), dma((peers,)), dma((2,)), dma((2,)),
            dma((column,)), dma((column,)), dma((column,)), dma((column,)), dma((2,)), dma((2,)),
        ],
        compiler_params=pltpu.CompilerParams(collective_id=0, has_side_effects=True),
        name="exchange",
    )(
        cell_counts, owners, block_slot, attitude, pay.reshape(10, DEV, 128), codes,
        star_partials, attitude_partials, observed, phase, knot_offset,
    )
    attitude_step, star_step = pl.pallas_call(
        sweep_kernel,
        out_shape=(
            jax.ShapeDtypeStruct((4, 256), f32),
            jax.ShapeDtypeStruct((5, CELLS_HERE * CS), f32),
        ),
        in_specs=[VMEM, VMEM],
        out_specs=(VMEM, VMEM),
        name="sweeps",
    )(reduced, steps)
    return (star_step, attitude_step)


def solution(mesh):
    both = ("cells", "tm")
    placed = (
        P(None, both), P(None, None, both), P(None, None, both), P(None, both), P(None, both), P(None, both),
        P(both), P(both, None, None), P(both, None),
    )
    return jax.shard_map(
        per_device, mesh=mesh, in_specs=placed, out_specs=(P(None, both), P(None, both)), check_vma=False
    )
```

```python
import functools

import jax
import jax.numpy as jnp
from jax import lax
from jax.experimental import pallas as pl
from jax.experimental.pallas import tpu as pltpu
from jax.sharding import PartitionSpec as P

NT, CS, KB, ITERS = 64, 128, 16, 6
NX, NY, NZ, NC = 4, 4, 8, 2
NP = NX * NY
DEV = NP * NZ * NC
QIN = NZ * NC
CELLS_HERE = 4
TR = CELLS_HERE * NT
ID_LANE = 63
MESH = pl.DeviceIdType.MESH
f32, bf16 = jnp.float32, jnp.bfloat16
PAIRS = [(m, n) for m in range(4) for n in range(m, 4)]
PAIR_OF = {pair: i for i, pair in enumerate(PAIRS)}
SHIFTS = [(t, i) for t in range(4) for i in range(4 - t)]
SHIFT_OF = {pair: i for i, pair in enumerate(SHIFTS)}
VMEM = pl.BlockSpec(memory_space=pltpu.VMEM)
SMEM = pl.BlockSpec(memory_space=pltpu.SMEM)


def place():
    cells, x = lax.axis_index("cells"), lax.axis_index("tm")
    z, y, c = cells // (NY * NC), (cells // NC) % NY, cells % NC
    return x, y, z, c


def device(x, y, z, c):
    return ((z * NY + y) * NC + c, x)


def remote(src, dst, send, recv, target):
    return pltpu.make_async_remote_copy(
        src_ref=src, dst_ref=dst, send_sem=send, recv_sem=recv, device_id=target, device_id_type=MESH
    )


def plane_peers(x, y, z, c):
    here = x * NY + y
    peers = []
    for i in range(1, NP):
        there = (here + i) % NP
        peers.append((there, device(there // NY, there % NY, z, c)))
    return peers


def column_peers(x, y, z, c):
    return [((z + i) % NZ, device(x, y, (z + i) % NZ, c)) for i in range(1, NZ)]


def greet(targets):
    barrier = pltpu.get_barrier_semaphore()
    for target in targets:
        pl.semaphore_signal(barrier, inc=1, device_id=target, device_id_type=MESH)
    return lambda: pl.semaphore_wait(barrier, len(targets))


def split(value):
    high = value.astype(bf16)
    low = (value - high.astype(f32)).astype(bf16)
    return high, low


def cholesky(entries, size):
    lower = [[None] * size for _ in range(size)]
    inverse = [None] * size
    for col in range(size):
        total = entries(col, col)
        for k in range(col):
            total = total - lower[col][k] * lower[col][k]
        inverse[col] = 1.0 / jnp.sqrt(total)
        for row in range(col + 1, size):
            acc = entries(row, col)
            for k in range(col):
                acc = acc - lower[row][k] * lower[col][k]
            lower[row][col] = acc * inverse[col]
    return lower, inverse


def substitute(lower, inverse, rhs, size):
    forward = []
    for row in range(size):
        acc = rhs[row]
        for k in range(row):
            acc = acc - lower[row][k] * forward[k]
        forward.append(acc * inverse[row])
    answer = [None] * size
    for row in reversed(range(size)):
        acc = forward[row]
        for k in range(row + 1, size):
            acc = acc - lower[k][row] * answer[k]
        answer[row] = acc * inverse[row]
    return answer


def spline(t, live):
    square = t * t
    cube = square * t
    rest = 1.0 - t
    return [
        rest * rest * rest * (1.0 / 6.0) * live,
        (3.0 * cube - 6.0 * square + 4.0) * (1.0 / 6.0) * live,
        (-3.0 * cube + 3.0 * square + 3.0 * t + 1.0) * (1.0 / 6.0) * live,
        cube * (1.0 / 6.0) * live,
    ]


def spread(rows, hits):
    value = jnp.zeros((16, 128), f32)
    for row, hit in reversed(list(zip(rows, hits))):
        value = jnp.where(hit, jnp.broadcast_to(row, (16, 128)), value)
    return value


def nt_dot(left, right):
    return lax.dot_general(left, right, (((1,), (1,)), ((), ())), preferred_element_type=f32)


def aligned(value):
    return pl.multiple_of(value, 8)


def main_kernel(
    counts, owners, slots, att_in, star, axis, observed, phase, offset,
    step_ref, out,
    att, cross, parts, offs, ownm, nrm, pay, sh, sl, table, first, sums, order, pick, grads, gpay, got, ggot,
    comb, part, zsum, zgot,
    zs, zr, ps, pr, cs, cr, ns, nr, gs, gr, ws, wr, us, ur, hs, hr,
):
    x, y, z, c = place()
    plane, column = plane_peers(x, y, z, c), column_peers(x, y, z, c)
    partner = device(x, y, z, 1 - c)
    rank = ((z * NY + y) * NC + c) * NX + x
    after, before = (rank + 1) % DEV, (rank + DEV - 1) % DEV
    right, left = (after // NX, after % NX), (before // NX, before % NX)
    all_here = greet([t for _, t in plane] + [t for _, t in column] + [partner, right, left])
    here = x * NY + y
    spot = (y * NC + c) * NX + x

    sub8 = lax.broadcasted_iota(jnp.int32, (8, 128), 0)
    lane8 = lax.broadcasted_iota(jnp.int32, (8, 128), 1)
    knot = lax.broadcasted_iota(jnp.int32, (16, 128), 0)
    att[z, spot, 0:4, :] = att_in[:, 0:128]
    att[z, spot, 4:8, :] = att_in[:, 128:256]

    for cell in range(CELLS_HERE):
        lanes = slice(cell * CS, (cell + 1) * CS)

        def prepare(g, acc, cell=cell, lanes=lanes):
            rows = pl.ds(aligned(g * 8), 8)
            at = cell * NT + g * 8
            live = jnp.where(sub8 + g * 8 < counts[cell], 1.0, 0.0)
            b = spline(phase[rows, lanes], live)
            offs[pl.ds(aligned(at), 8), :] = offset[rows, lanes]
            for n, (shift, i) in enumerate(SHIFTS):
                cross[pl.ds(aligned(n * TR + at), 8), :] = b[i] * b[i + shift]
            for m in range(4):
                parts[pl.ds(aligned(m * TR + at), 8), :] = axis[m, rows, lanes]
                parts[pl.ds(aligned((4 + m) * TR + at), 8), :] = b[m]
            for jj in range(8):
                ownm[pl.ds(at + jj, 1), :] = jnp.full((1, 128), owners[cell, g * 8 + jj], jnp.int32)
            p = [star[m, rows, lanes] * live for m in range(5)]
            terms = [p[i] * p[j] for i in range(5) for j in range(i + 1)]
            return tuple(s + term for s, term in zip(acc, terms))

        acc = lax.fori_loop(0, NT // 8, prepare, tuple(jnp.zeros((8, 128), f32) for _ in range(15)))
        for n in range(15):
            sums[n:n + 1, lanes] = jnp.sum(acc[n], axis=0, keepdims=True)

    def spreads(g, carry):
        pieces = []
        for jj in range(8):
            at = g * 8 + jj
            gap = knot - jnp.broadcast_to(offs[pl.ds(at, 1), :], (16, 128))
            pieces.append(spread([parts[pl.ds((4 + i) * TR + at, 1), :] for i in range(4)], [gap == i for i in range(4)]))
        high, low = split(jnp.concatenate(pieces, axis=0))
        where = pl.ds(pl.multiple_of(g * 128, 128), 128)
        sh[where, :] = high
        sl[where, :] = low
        return carry

    lax.fori_loop(0, TR // 8, spreads, 0)

    def entry(i, j):
        n = i * (i + 1) // 2 + j
        return sums[n:n + 1, :] + (1.0 if i == j else 0.0)

    lower, inverse = cholesky(entry, 5)

    all_here()
    mine = att.at[z, spot]
    gather_z = [remote(mine, mine, zs.at[i], zr.at[i], t) for i, (_, t) in enumerate(column)]
    for copy in gather_z:
        copy.start()

    def normals(g, carry):
        for jj in range(16):
            at = g * 16 + jj
            gap = knot - jnp.broadcast_to(offs[pl.ds(at, 1), :], (16, 128))
            hits = [gap == i for i in range(4)]
            right = jnp.concatenate(
                [
                    spread([cross[pl.ds(SHIFT_OF[(s, i)] * TR + at, 1), :] for i in range(4 - s)], hits)
                    for s in range(4)
                ],
                axis=0,
            )
            a = [jnp.broadcast_to(parts[pl.ds(m * TR + at, 1), :], (8, 128)) for m in range(4)]
            top = jnp.where(sub8 == 4, a[1], a[0]) * jnp.where(
                sub8 == 0, a[0], jnp.where(sub8 == 2, a[2], jnp.where(sub8 == 3, a[3], a[1]))
            )
            bottom = jnp.where(sub8 < 2, a[1], jnp.where(sub8 == 4, a[3], a[2])) * jnp.where(
                (sub8 == 0) | (sub8 == 2), a[2], a[3]
            )
            rh, rl = split(right)
            lh, ll = split(jnp.concatenate([top, bottom], axis=0))
            big = nt_dot(jnp.concatenate([lh, ll], axis=0), jnp.concatenate([rh, rl], axis=0))
            total = big[0:16] + big[16:32]
            total = total + pltpu.roll(total, 64, 1)
            packed = jnp.where(lane8 < 64, total[0:8], total[8:16])
            slot = slots[lax.shift_right_logical(g, 2), (g & 3) * 16 + jj]
            packed = jnp.where((sub8 == 0) & (lane8 == ID_LANE), slot.astype(f32), packed)
            nrm[pl.ds(at, 5, stride=TR), :] = packed[0:5]
        return carry

    lax.fori_loop(0, 7, normals, 0)

    for copy in gather_z:
        copy.wait_recv()
    mine = att.at[:, spot]
    gather_p = [remote(mine, mine, ps.at[i], pr.at[i], t) for i, (_, t) in enumerate(plane)]
    for copy in gather_p:
        copy.start()

    lax.fori_loop(7, TR // 16, normals, 0)

    owner = jnp.concatenate([ownm[...], ownm[...]], axis=1)
    other = owner.astype(f32).T
    left_of = lax.broadcasted_iota(jnp.int32, (TR, TR), 1) < lax.broadcasted_iota(jnp.int32, (TR, TR), 0)
    same = jnp.where((owner.astype(f32) == other) & left_of, 1.0, 0.0)
    place_in = jnp.sum(same, axis=1, keepdims=True).astype(jnp.int32)
    q = ((owner & 3) << 6) | ((owner & 24) << 1) | ((owner & 4) << 1) | lax.shift_right_logical(owner, 5)
    code = q + place_in * DEV
    target = lax.broadcasted_iota(jnp.int32, (TR, DEV), 1)
    for s in range(2):
        order[s * DEV:(s + 1) * DEV, :] = jnp.where(code == target + s * DEV, 1.0, 0.0).T.astype(bf16)

    def doubled(matrix, data):
        big = jnp.dot(matrix, jnp.concatenate(split(data), axis=1), preferred_element_type=f32)
        return big[:, 0:128] + big[:, 128:256]

    for r in range(5):
        sorted_rows = doubled(order[...], nrm[r * TR:(r + 1) * TR, :])
        for s in range(2):
            pay[r, s] = sorted_rows[s * DEV:(s + 1) * DEV]

    for copy in gather_p:
        copy.wait_recv()
    gather_c = []
    for i in range(NY):
        mine = att.at[:, pl.ds(i * NC * NX + c * NX, NX)]
        gather_c.append(remote(mine, mine, cs.at[i], cr.at[i], partner))
    for copy in gather_c:
        copy.start()
    terms = [
        [
            remote(pay.at[r, :, pl.ds(p * QIN, QIN), :], got.at[r, here], ns.at[r, i], nr.at[r, i], t)
            for i, (p, t) in enumerate(plane)
        ]
        for r in range(5)
    ]
    for group in terms:
        for copy in group:
            copy.start()
    got[:, here] = pay[:, :, pl.ds(pl.multiple_of(here * QIN, QIN), QIN), :]
    for copy in gather_c:
        copy.wait_recv()

    lane4 = lax.broadcasted_iota(jnp.int32, (4, 128), 1) // KB

    def choose(g, carry):
        cell, base = lax.shift_right_logical(g, 3), (g & 7) * 8
        for jj in range(8):
            owner, slot = owners[cell, base + jj], slots[cell, base + jj]
            rows4 = att[lax.shift_right_logical(owner, 5), owner & 31, pl.ds((slot & 8) >> 1, 4), :]
            table[pl.ds(g * 32 + jj, 4, stride=8), :] = jnp.where(lane4 == (slot & 7), rows4, 0.0)
        return carry

    lax.fori_loop(0, TR // 8, choose, 0)

    lane32 = lax.broadcasted_iota(jnp.int32, (32, 128), 1)
    row32 = lax.broadcasted_iota(jnp.int32, (32, 128), 0)
    own = (lane32 // KB) == (row32 % 8)

    def fold(value):
        for shift in (64, 32, 16):
            value = value + pltpu.roll(value, shift, 1)
        return value

    for cell in range(CELLS_HERE):
        lanes = slice(cell * CS, (cell + 1) * CS)

        def predict(g, acc, cell=cell, lanes=lanes):
            rows = pl.ds(aligned(g * 8), 8)
            gg = cell * 8 + g
            live = jnp.where(sub8 + g * 8 < counts[cell], 1.0, 0.0)
            coeff = jnp.where(own, fold(table[pl.ds(aligned(gg * 32), 32), :]), 0.0)
            high, low = split(coeff)
            where = pl.ds(pl.multiple_of(gg * 128, 128), 128)
            big = jnp.dot(jnp.concatenate([high, low], axis=0), sh[where, :], preferred_element_type=f32)
            fit = big[0:32] + big[32:64] + jnp.dot(high, sl[where, :], preferred_element_type=f32)
            value = live * observed[rows, lanes]
            for m in range(4):
                value = value - axis[m, rows, lanes] * fit[m * 8:(m + 1) * 8]
            first[pl.ds(aligned(gg * 8), 8), :] = value
            return tuple(s + star[n, rows, lanes] * value for n, s in enumerate(acc))

        acc = lax.fori_loop(0, NT // 8, predict, tuple(jnp.zeros((8, 128), f32) for _ in range(5)), unroll=2)
        for n in range(5):
            sums[15 + n:16 + n, lanes] = jnp.sum(acc[n], axis=0, keepdims=True)

    steps = substitute(lower, inverse, [sums[15 + n:16 + n, :] for n in range(5)], 5)
    for n in range(5):
        step_ref[n:n + 1, :] = steps[n]

    for cell in range(CELLS_HERE):
        lanes = slice(cell * CS, (cell + 1) * CS)

        def gradients(g, carry, cell=cell, lanes=lanes):
            rows = pl.ds(aligned(g * 8), 8)
            gg = cell * 8 + g
            live = jnp.where(sub8 + g * 8 < counts[cell], 1.0, 0.0)
            fitted = star[0, rows, lanes] * step_ref[0:1, lanes]
            for n in range(1, 5):
                fitted = fitted + star[n, rows, lanes] * step_ref[n:n + 1, lanes]
            second = first[pl.ds(aligned(gg * 8), 8), :] - live * fitted
            high, low = split(jnp.concatenate([axis[m, rows, lanes] * second for m in range(4)], axis=0))
            where = pl.ds(pl.multiple_of(gg * 128, 128), 128)
            big = nt_dot(jnp.concatenate([high, low], axis=0), sh[where, :])
            total = big[0:32] + big[32:64] + nt_dot(high, sl[where, :])
            total = fold(jnp.where(own, total, 0.0))
            grad = jnp.zeros((8, 128), f32)
            for m in range(4):
                grad = jnp.where((lane8 // KB) % 4 == m, total[m * 8:(m + 1) * 8], grad)
            grads[pl.ds(aligned(gg * 8), 8), :] = grad
            return carry

        lax.fori_loop(0, NT // 8, gradients, 0, unroll=2)

    lane = lax.broadcasted_iota(jnp.int32, (TR, 128), 1)
    placed = doubled(order[...], grads[...])
    gpay[...] = jnp.where(lane < 64, placed[0:DEV], placed[DEV:2 * DEV])
    gterms = [
        remote(gpay.at[pl.ds(p * QIN, QIN), :], ggot.at[here], gs.at[i], gr.at[i], t) for i, (p, t) in enumerate(plane)
    ]
    for copy in gterms:
        copy.start()
    ggot[here] = gpay[pl.ds(pl.multiple_of(here * QIN, QIN), QIN), :]

    rows = NP * QIN
    cols = QIN * KB
    half = NZ * KB
    keep = pl.ds(pl.multiple_of(c * half, half), half)
    give = pl.ds(pl.multiple_of((1 - c) * half, half), half)
    swaps = [remote(comb.at[r, give, :], part.at[r], ws.at[r], wr.at[r], partner) for r in range(6)]
    along = [
        [
            remote(zsum.at[r, pl.ds(zz * KB, KB), :], zgot.at[r, z], us.at[r, i], ur.at[r, i], t)
            for i, (zz, t) in enumerate(column)
        ]
        for r in range(6)
    ]

    def forward(r):
        swaps[r].wait_recv()
        zsum[r] = comb[r, keep, :] + part[r]
        for copy in along[r]:
            copy.start()
        zgot[r, z] = zsum[r, pl.ds(pl.multiple_of(z * KB, KB), KB), :]

    for r in range(6):
        for copy in terms[r] if r < 5 else gterms:
            copy.wait_recv()
        if r == 0:
            row = lax.broadcasted_iota(jnp.int32, (rows, cols), 0)
            col = lax.broadcasted_iota(jnp.int32, (rows, cols), 1)
            local = (col - (row % QIN) * KB).astype(f32)
            for s in range(2):
                ids = got[0, :, s, :, :].reshape(rows, 128)[:, ID_LANE:ID_LANE + 1]
                pick[:, s * rows:(s + 1) * rows] = jnp.where(local == ids, 1.0, 0.0).T.astype(bf16)
        if r < 5:
            data = jnp.concatenate([got[r, :, s, :, :].reshape(rows, 128) for s in range(2)], axis=0)
        else:
            both = ggot[...].reshape(rows, 128)
            data = jnp.concatenate([jnp.where(lane < 64, both, 0.0), jnp.where(lane < 64, 0.0, both)], axis=0)
        comb[r] = doubled(pick[...], data)
        swaps[r].start()
        if r > 0:
            forward(r - 1)
    forward(5)
    for group in along:
        for copy in group:
            copy.wait_recv()
    for r in range(6):
        total = zgot[r, 0]
        for i in range(1, NZ):
            total = total + zgot[r, i]
        out[r, 8:24, :] = total
    halo = [
        remote(out.at[:, 16:24, :], out.at[:, 0:8, :], hs.at[0], hr.at[0], right),
        remote(out.at[:, 8:16, :], out.at[:, 24:32, :], hs.at[1], hr.at[1], left),
    ]
    for copy in halo:
        copy.start()
    for copy in gather_z + gather_p + gather_c + sum(terms, []) + gterms + swaps + sum(along, []):
        copy.wait_send()
    for copy in halo:
        copy.wait()


def sweep_kernel(red, steps, out, steps_out):
    steps_out[...] = steps[...]
    rank = lax.axis_index("cells") * NX + lax.axis_index("tm")
    shape = (32, 128)
    row = lax.broadcasted_iota(jnp.int32, shape, 0)
    lane = lax.broadcasted_iota(jnp.int32, shape, 1)
    k = lane % KB
    beyond = ((row == 7) & (rank == 0)) | ((row == 24) & (rank == DEV - 1))
    valid = jnp.where(beyond, 0.0, 1.0)
    ahead, behind = {}, {}
    for n in range(10):
        comp = red[n % 5]
        start = (n // 5) * 64
        for t in range(4):
            value = jnp.take_along_axis(comp, start + t * 16 + k, axis=1)
            ahead[n, t] = jnp.where(k + t < KB, value, 0.0) if t else value
            if t:
                value = jnp.take_along_axis(comp, start + t * 16 + (k + KB - t) % KB, axis=1)
                behind[n, t] = jnp.where(k >= t, value, 0.0)
    for n, (i, j) in enumerate(PAIRS):
        if i == j:
            ahead[n, 0] = ahead[n, 0] + 34.0
    fold = red[5]
    fold = fold + pltpu.roll(fold, 64, 1)
    gradient = [jnp.take_along_axis(fold, m * KB + k, axis=1) for m in range(4)]

    def pair(i, j):
        return PAIR_OF[(min(i, j), max(i, j))]

    lower, inverse = cholesky(lambda i, j: ahead[pair(i, j), 0], 4)
    x = [0.5 * v * valid for v in substitute(lower, inverse, gradient, 4)]
    for _ in range(ITERS - 1):
        misfit = list(gradient)
        for n in range(4):
            up = {t: pltpu.roll(x[n], 128 - t, 1) for t in (1, 2, 3)}
            down = {t: pltpu.roll(x[n], t, 1) for t in (1, 2, 3)}
            for m in range(4):
                p = pair(m, n)
                acc = ahead[p, 0] * x[n]
                for t in (1, 2, 3):
                    acc = acc + ahead[p, t] * up[t] + behind[p, t] * down[t]
                misfit[m] = misfit[m] - acc
            before = jnp.where(k == 0, pltpu.roll(down[1], 1, 0), down[1])
            after = jnp.where(k == KB - 1, pltpu.roll(up[1], 31, 0), up[1])
            misfit[n] = misfit[n] + 16.0 * (before + after)
        x = [(v + 0.5 * w) * valid for v, w in zip(x, substitute(lower, inverse, misfit, 4))]
    sub8 = lax.broadcasted_iota(jnp.int32, (8, 128), 0)
    keep = sub8 == lax.broadcasted_iota(jnp.int32, (8, 128), 1) // KB
    for m in range(4):
        for h in range(2):
            part = jnp.where(keep, x[m][8 + h * 8:16 + h * 8], 0.0)
            out[m:m + 1, h * 128:(h + 1) * 128] = jnp.sum(part, axis=0, keepdims=True)


def per_device(
    attitude, star_partials, attitude_partials, observed, phase, knot_offset, cell_counts, interval_owner, block_slot
):
    dma = pltpu.SemaphoreType.DMA
    owners = interval_owner.reshape(CELLS_HERE, NT)
    peers, column = NP - 1, NZ - 1
    steps, reduced = pl.pallas_call(
        main_kernel,
        out_shape=(
            jax.ShapeDtypeStruct((5, CELLS_HERE * CS), f32),
            jax.ShapeDtypeStruct((6, 32, 128), f32),
        ),
        in_specs=[SMEM, SMEM, SMEM] + [VMEM] * 6,
        out_specs=(VMEM, VMEM),
        scratch_shapes=[
            pltpu.VMEM((NZ, NY * NC * NX, 8, 128), f32),
            pltpu.VMEM((10 * TR, 128), f32),
            pltpu.VMEM((8 * TR, 128), f32),
            pltpu.VMEM((TR, 128), jnp.int32),
            pltpu.VMEM((TR, 128), jnp.int32),
            pltpu.VMEM((5 * TR, 128), f32),
            pltpu.VMEM((5, 2, DEV, 128), f32),
            pltpu.VMEM((TR * KB, 128), bf16),
            pltpu.VMEM((TR * KB, 128), bf16),
            pltpu.VMEM((4 * TR, 128), f32),
            pltpu.VMEM((TR, 128), f32),
            pltpu.VMEM((24, CELLS_HERE * CS), f32),
            pltpu.VMEM((2 * DEV, TR), bf16),
            pltpu.VMEM((QIN * KB, 2 * NP * QIN), bf16),
            pltpu.VMEM((TR, 128), f32),
            pltpu.VMEM((DEV, 128), f32),
            pltpu.VMEM((5, NP, 2, QIN, 128), f32),
            pltpu.VMEM((NP, QIN, 128), f32),
            pltpu.VMEM((6, QIN * KB, 128), f32),
            pltpu.VMEM((6, NZ * KB, 128), f32),
            pltpu.VMEM((6, NZ * KB, 128), f32),
            pltpu.VMEM((6, NZ, KB, 128), f32),
            dma((column,)), dma((column,)), dma((peers,)), dma((peers,)), dma((NY,)), dma((NY,)),
            dma((5, peers)), dma((5, peers)), dma((peers,)), dma((peers,)), dma((6,)), dma((6,)),
            dma((6, column)), dma((6, column)), dma((2,)), dma((2,)),
        ],
        compiler_params=pltpu.CompilerParams(collective_id=0, has_side_effects=True),
        name="exchange",
    )(
        cell_counts, owners, block_slot, attitude,
        star_partials, attitude_partials, observed, phase, knot_offset,
    )
    attitude_step, star_step = pl.pallas_call(
        sweep_kernel,
        out_shape=(
            jax.ShapeDtypeStruct((4, 256), f32),
            jax.ShapeDtypeStruct((5, CELLS_HERE * CS), f32),
        ),
        in_specs=[VMEM, VMEM],
        out_specs=(VMEM, VMEM),
        name="sweeps",
    )(reduced, steps)
    return (star_step, attitude_step)


def solution(mesh):
    both = ("cells", "tm")
    placed = (
        P(None, both), P(None, None, both), P(None, None, both), P(None, both), P(None, both), P(None, both),
        P(both), P(both, None, None), P(both, None),
    )
    return jax.shard_map(
        per_device, mesh=mesh, in_specs=placed, out_specs=(P(None, both), P(None, both)), check_vma=False
    )
```

```python
import functools

import jax
import jax.numpy as jnp
from jax import lax
from jax.experimental import pallas as pl
from jax.experimental.pallas import tpu as pltpu
from jax.sharding import PartitionSpec as P

NT, CS, KB, ITERS = 64, 128, 16, 6
NX, NY, NZ, NC = 4, 4, 8, 2
NP = NX * NY
DEV = NP * NZ * NC
QIN = NZ * NC
CELLS_HERE = 4
TR = CELLS_HERE * NT
ID_LANE = 63
MESH = pl.DeviceIdType.MESH
f32, bf16 = jnp.float32, jnp.bfloat16
PAIRS = [(m, n) for m in range(4) for n in range(m, 4)]
PAIR_OF = {pair: i for i, pair in enumerate(PAIRS)}
SHIFTS = [(t, i) for t in range(4) for i in range(4 - t)]
SHIFT_OF = {pair: i for i, pair in enumerate(SHIFTS)}
VMEM = pl.BlockSpec(memory_space=pltpu.VMEM)
SMEM = pl.BlockSpec(memory_space=pltpu.SMEM)


def place():
    cells, x = lax.axis_index("cells"), lax.axis_index("tm")
    z, y, c = lax.div(cells, NY * NC), lax.rem(lax.div(cells, NC), NY), lax.rem(cells, NC)
    return x, y, z, c


def device(x, y, z, c):
    return ((z * NY + y) * NC + c, x)


def remote(src, dst, send, recv, target):
    return pltpu.make_async_remote_copy(
        src_ref=src, dst_ref=dst, send_sem=send, recv_sem=recv, device_id=target, device_id_type=MESH
    )


def plane_peers(x, y, z, c):
    xs = [x] + [lax.rem(x + d, NX) for d in range(1, NX)]
    ys = [y] + [lax.rem(y + d, NY) for d in range(1, NY)]
    return [(i * NY + j, device(i, j, z, c)) for i in xs for j in ys][1:]


def column_peers(x, y, z, c):
    return [(zz, device(x, y, zz, c)) for zz in [lax.rem(z + i, NZ) for i in range(1, NZ)]]


def greet(targets):
    barrier = pltpu.get_barrier_semaphore()
    for target in targets:
        pl.semaphore_signal(barrier, inc=1, device_id=target, device_id_type=MESH)
    return lambda: pl.semaphore_wait(barrier, len(targets))


def split(value):
    high = value.astype(bf16)
    low = (value - high.astype(f32)).astype(bf16)
    return high, low


def cholesky(entries, size):
    lower = [[None] * size for _ in range(size)]
    inverse = [None] * size
    for col in range(size):
        total = entries(col, col)
        for k in range(col):
            total = total - lower[col][k] * lower[col][k]
        inverse[col] = 1.0 / jnp.sqrt(total)
        for row in range(col + 1, size):
            acc = entries(row, col)
            for k in range(col):
                acc = acc - lower[row][k] * lower[col][k]
            lower[row][col] = acc * inverse[col]
    return lower, inverse


def substitute(lower, inverse, rhs, size):
    forward = []
    for row in range(size):
        acc = rhs[row]
        for k in range(row):
            acc = acc - lower[row][k] * forward[k]
        forward.append(acc * inverse[row])
    answer = [None] * size
    for row in reversed(range(size)):
        acc = forward[row]
        for k in range(row + 1, size):
            acc = acc - lower[k][row] * answer[k]
        answer[row] = acc * inverse[row]
    return answer


def spline(t, live):
    square = t * t
    cube = square * t
    rest = 1.0 - t
    return [
        rest * rest * rest * (1.0 / 6.0) * live,
        (3.0 * cube - 6.0 * square + 4.0) * (1.0 / 6.0) * live,
        (-3.0 * cube + 3.0 * square + 3.0 * t + 1.0) * (1.0 / 6.0) * live,
        cube * (1.0 / 6.0) * live,
    ]


def spread(rows, hits):
    value = jnp.zeros((16, 128), f32)
    for row, hit in reversed(list(zip(rows, hits))):
        value = jnp.where(hit, jnp.broadcast_to(row, (16, 128)), value)
    return value


def nt_dot(left, right):
    return lax.dot_general(left, right, (((1,), (1,)), ((), ())), preferred_element_type=f32)


def aligned(value):
    return pl.multiple_of(value, 8)


def main_kernel(
    counts, owners, slots, att_in, star, axis, observed, phase, offset,
    step_ref, out,
    att, cross, parts, offs, ownm, nrm, pay, sh, sl, table, first, sums, order, pick, grads, gpay, got, ggot,
    comb, part, zsum, zgot,
    zs, zr, ps, pr, cs, cr, ns, nr, gs, gr, ws, wr, us, ur, hs, hr,
):
    x, y, z, c = place()
    plane, column = plane_peers(x, y, z, c), column_peers(x, y, z, c)
    partner = device(x, y, z, 1 - c)
    rank = ((z * NY + y) * NC + c) * NX + x
    after, before = lax.rem(rank + 1, DEV), lax.rem(rank + DEV - 1, DEV)
    right, left = [(lax.div(d, NX), lax.rem(d, NX)) for d in (after, before)]
    all_here = greet([t for _, t in plane] + [t for _, t in column] + [partner, right, left])
    here = x * NY + y
    spot = (y * NC + c) * NX + x

    sub8 = lax.broadcasted_iota(jnp.int32, (8, 128), 0)
    lane8 = lax.broadcasted_iota(jnp.int32, (8, 128), 1)
    knot = lax.broadcasted_iota(jnp.int32, (16, 128), 0)
    att[z, spot, 0:4, :] = att_in[:, 0:128]
    att[z, spot, 4:8, :] = att_in[:, 128:256]

    for cell in range(CELLS_HERE):
        lanes = slice(cell * CS, (cell + 1) * CS)

        def prepare(g, acc, cell=cell, lanes=lanes):
            rows = pl.ds(aligned(g * 8), 8)
            at = cell * NT + g * 8
            live = jnp.where(sub8 + g * 8 < counts[cell], 1.0, 0.0)
            b = spline(phase[rows, lanes], live)
            offs[pl.ds(aligned(at), 8), :] = offset[rows, lanes]
            for n, (shift, i) in enumerate(SHIFTS):
                cross[pl.ds(aligned(n * TR + at), 8), :] = b[i] * b[i + shift]
            for m in range(4):
                parts[pl.ds(aligned(m * TR + at), 8), :] = axis[m, rows, lanes]
                parts[pl.ds(aligned((4 + m) * TR + at), 8), :] = b[m]
            for jj in range(8):
                ownm[pl.ds(at + jj, 1), :] = jnp.full((1, 128), owners[cell, g * 8 + jj], jnp.int32)
            p = [star[m, rows, lanes] * live for m in range(5)]
            terms = [p[i] * p[j] for i in range(5) for j in range(i + 1)]
            return tuple(s + term for s, term in zip(acc, terms))

        acc = lax.fori_loop(0, NT // 8, prepare, tuple(jnp.zeros((8, 128), f32) for _ in range(15)))
        for n in range(15):
            sums[n:n + 1, lanes] = jnp.sum(acc[n], axis=0, keepdims=True)

    def sides(at):
        gap = knot - jnp.broadcast_to(offs[pl.ds(at, 1), :], (16, 128))
        hits = [gap == i for i in range(4)]
        right = jnp.concatenate(
            [
                spread([cross[pl.ds(SHIFT_OF[(s, i)] * TR + at, 1), :] for i in range(4 - s)], hits)
                for s in range(4)
            ],
            axis=0,
        )
        a = [jnp.broadcast_to(parts[pl.ds(m * TR + at, 1), :], (8, 128)) for m in range(4)]
        top = jnp.where(sub8 == 4, a[1], a[0]) * jnp.where(
            sub8 == 0, a[0], jnp.where(sub8 == 2, a[2], jnp.where(sub8 == 3, a[3], a[1]))
        )
        bottom = jnp.where(sub8 < 2, a[1], jnp.where(sub8 == 4, a[3], a[2])) * jnp.where(
            (sub8 == 0) | (sub8 == 2), a[2], a[3]
        )
        rh, rl = split(right)
        lh, ll = split(jnp.concatenate([top, bottom], axis=0))
        return jnp.concatenate([lh, ll], axis=0), jnp.concatenate([rh, rl], axis=0)

    def finish(at, slot, big):
        total = big[0:16] + big[16:32]
        total = total + pltpu.roll(total, 64, 1)
        packed = jnp.where(lane8 < 64, total[0:8], total[8:16])
        packed = jnp.where((sub8 == 0) & (lane8 == ID_LANE), slot.astype(f32), packed)
        nrm[pl.ds(at, 5, stride=TR), :] = packed[0:5]

    blank = jnp.zeros((32, 128), bf16)

    def normals(g, carry):
        for jj in range(0, 32, 2):
            at = g * 32 + jj
            left0, right0 = sides(at)
            left1, right1 = sides(at + 1)
            left = jnp.concatenate(
                [jnp.concatenate([left0, blank], axis=1), jnp.concatenate([blank, left1], axis=1)], axis=0
            )
            big = nt_dot(left, jnp.concatenate([right0, right1], axis=1))
            for e in range(2):
                slot = slots[lax.shift_right_logical(g, 1), (g & 1) * 32 + jj + e]
                finish(at + e, slot, big[e * 32:(e + 1) * 32])
        return carry

    lax.fori_loop(0, 4, normals, 0)

    all_here()
    mine = att.at[z, spot]
    gather_z = [remote(mine, mine, zs.at[i], zr.at[i], t) for i, (_, t) in enumerate(column)]
    for copy in gather_z:
        copy.start()

    lax.fori_loop(4, TR // 32, normals, 0)

    owner = jnp.concatenate([ownm[...], ownm[...]], axis=1)
    other = owner.astype(f32).T
    left_of = lax.broadcasted_iota(jnp.int32, (TR, TR), 1) < lax.broadcasted_iota(jnp.int32, (TR, TR), 0)
    same = jnp.where((owner.astype(f32) == other) & left_of, 1.0, 0.0)
    place_in = jnp.sum(same, axis=1, keepdims=True).astype(jnp.int32)
    q = ((owner & 3) << 6) | ((owner & 24) << 1) | ((owner & 4) << 1) | lax.shift_right_logical(owner, 5)
    code = q + place_in * DEV
    target = lax.broadcasted_iota(jnp.int32, (TR, DEV), 1)
    for s in range(2):
        order[s * DEV:(s + 1) * DEV, :] = jnp.where(code == target + s * DEV, 1.0, 0.0).T.astype(bf16)

    for copy in gather_z:
        copy.wait_recv()
    mine = att.at[:, spot]
    gather_p = [remote(mine, mine, ps.at[i], pr.at[i], t) for i, (_, t) in enumerate(plane)]
    for copy in gather_p:
        copy.start()

    def doubled(matrix, data):
        big = jnp.dot(matrix, jnp.concatenate(split(data), axis=1), preferred_element_type=f32)
        return big[:, 0:128] + big[:, 128:256]

    terms = []
    for r in range(5):
        sorted_rows = doubled(order[...], nrm[r * TR:(r + 1) * TR, :])
        for s in range(2):
            pay[r, s] = sorted_rows[s * DEV:(s + 1) * DEV]
        terms.append([
            remote(pay.at[r, :, pl.ds(p * QIN, QIN), :], got.at[r, here], ns.at[r, i], nr.at[r, i], t)
            for i, (p, t) in enumerate(plane)
        ])
        for copy in terms[r]:
            copy.start()
    got[:, here] = pay[:, :, pl.ds(pl.multiple_of(here * QIN, QIN), QIN), :]

    def spreads(g, carry):
        pieces = []
        for jj in range(8):
            at = g * 8 + jj
            gap = knot - jnp.broadcast_to(offs[pl.ds(at, 1), :], (16, 128))
            pieces.append(spread([parts[pl.ds((4 + i) * TR + at, 1), :] for i in range(4)], [gap == i for i in range(4)]))
        high, low = split(jnp.concatenate(pieces, axis=0))
        where = pl.ds(pl.multiple_of(g * 128, 128), 128)
        sh[where, :] = high
        sl[where, :] = low
        return carry

    lax.fori_loop(0, TR // 8, spreads, 0)

    def entry(i, j):
        n = i * (i + 1) // 2 + j
        return sums[n:n + 1, :] + (1.0 if i == j else 0.0)

    lower, inverse = cholesky(entry, 5)

    for copy in gather_p:
        copy.wait_recv()
    gather_c = []
    for i in range(NY):
        mine = att.at[:, pl.ds(i * NC * NX + c * NX, NX)]
        gather_c.append(remote(mine, mine, cs.at[i], cr.at[i], partner))
    for copy in gather_c:
        copy.start()
    for copy in gather_c:
        copy.wait_recv()

    lane4 = lax.broadcasted_iota(jnp.int32, (4, 128), 1) // KB

    def choose(g, carry):
        cell, base = lax.shift_right_logical(g, 3), (g & 7) * 8
        for jj in range(8):
            owner, slot = owners[cell, base + jj], slots[cell, base + jj]
            rows4 = att[lax.shift_right_logical(owner, 5), owner & 31, pl.ds((slot & 8) >> 1, 4), :]
            table[pl.ds(g * 32 + jj, 4, stride=8), :] = jnp.where(lane4 == (slot & 7), rows4, 0.0)
        return carry

    lax.fori_loop(0, TR // 8, choose, 0)

    lane32 = lax.broadcasted_iota(jnp.int32, (32, 128), 1)
    row32 = lax.broadcasted_iota(jnp.int32, (32, 128), 0)
    own = (lane32 // KB) == (row32 % 8)

    def fold(value):
        for shift in (64, 32, 16):
            value = value + pltpu.roll(value, shift, 1)
        return value

    for cell in range(CELLS_HERE):
        lanes = slice(cell * CS, (cell + 1) * CS)

        def predict(g, acc, cell=cell, lanes=lanes):
            rows = pl.ds(aligned(g * 8), 8)
            gg = cell * 8 + g
            live = jnp.where(sub8 + g * 8 < counts[cell], 1.0, 0.0)
            coeff = jnp.where(own, fold(table[pl.ds(aligned(gg * 32), 32), :]), 0.0)
            high, low = split(coeff)
            where = pl.ds(pl.multiple_of(gg * 128, 128), 128)
            big = jnp.dot(jnp.concatenate([high, low], axis=0), sh[where, :], preferred_element_type=f32)
            fit = big[0:32] + big[32:64] + jnp.dot(high, sl[where, :], preferred_element_type=f32)
            value = live * observed[rows, lanes]
            for m in range(4):
                value = value - axis[m, rows, lanes] * fit[m * 8:(m + 1) * 8]
            first[pl.ds(aligned(gg * 8), 8), :] = value
            return tuple(s + star[n, rows, lanes] * value for n, s in enumerate(acc))

        acc = lax.fori_loop(0, NT // 8, predict, tuple(jnp.zeros((8, 128), f32) for _ in range(5)), unroll=2)
        for n in range(5):
            sums[15 + n:16 + n, lanes] = jnp.sum(acc[n], axis=0, keepdims=True)

    steps = substitute(lower, inverse, [sums[15 + n:16 + n, :] for n in range(5)], 5)
    for n in range(5):
        step_ref[n:n + 1, :] = steps[n]

    for cell in range(CELLS_HERE):
        lanes = slice(cell * CS, (cell + 1) * CS)

        def gradients(g, carry, cell=cell, lanes=lanes):
            rows = pl.ds(aligned(g * 8), 8)
            gg = cell * 8 + g
            live = jnp.where(sub8 + g * 8 < counts[cell], 1.0, 0.0)
            fitted = star[0, rows, lanes] * step_ref[0:1, lanes]
            for n in range(1, 5):
                fitted = fitted + star[n, rows, lanes] * step_ref[n:n + 1, lanes]
            second = first[pl.ds(aligned(gg * 8), 8), :] - live * fitted
            high, low = split(jnp.concatenate([axis[m, rows, lanes] * second for m in range(4)], axis=0))
            where = pl.ds(pl.multiple_of(gg * 128, 128), 128)
            big = nt_dot(jnp.concatenate([high, low], axis=0), sh[where, :])
            total = big[0:32] + big[32:64] + nt_dot(high, sl[where, :])
            total = fold(jnp.where(own, total, 0.0))
            grad = jnp.zeros((8, 128), f32)
            for m in range(4):
                grad = jnp.where((lane8 // KB) % 4 == m, total[m * 8:(m + 1) * 8], grad)
            grads[pl.ds(aligned(gg * 8), 8), :] = grad
            return carry

        lax.fori_loop(0, NT // 8, gradients, 0, unroll=2)

    lane = lax.broadcasted_iota(jnp.int32, (TR, 128), 1)
    placed = doubled(order[...], grads[...])
    gpay[...] = jnp.where(lane < 64, placed[0:DEV], placed[DEV:2 * DEV])
    gterms = [
        remote(gpay.at[pl.ds(p * QIN, QIN), :], ggot.at[here], gs.at[i], gr.at[i], t) for i, (p, t) in enumerate(plane)
    ]
    for copy in gterms:
        copy.start()
    ggot[here] = gpay[pl.ds(pl.multiple_of(here * QIN, QIN), QIN), :]

    rows = NP * QIN
    cols = QIN * KB
    half = NZ * KB
    keep = pl.ds(pl.multiple_of(c * half, half), half)
    give = pl.ds(pl.multiple_of((1 - c) * half, half), half)
    swaps = [remote(comb.at[r, give, :], part.at[r], ws.at[r], wr.at[r], partner) for r in range(6)]
    along = [
        [
            remote(zsum.at[r, pl.ds(zz * KB, KB), :], zgot.at[r, z], us.at[r, i], ur.at[r, i], t)
            for i, (zz, t) in enumerate(column)
        ]
        for r in range(6)
    ]

    def forward(r):
        swaps[r].wait_recv()
        zsum[r] = comb[r, keep, :] + part[r]
        for copy in along[r]:
            copy.start()
        zgot[r, z] = zsum[r, pl.ds(pl.multiple_of(z * KB, KB), KB), :]

    for r in range(6):
        for copy in terms[r] if r < 5 else gterms:
            copy.wait_recv()
        if r == 0:
            row = lax.broadcasted_iota(jnp.int32, (rows, cols), 0)
            col = lax.broadcasted_iota(jnp.int32, (rows, cols), 1)
            local = (col - (row % QIN) * KB).astype(f32)
            for s in range(2):
                ids = got[0, :, s, :, :].reshape(rows, 128)[:, ID_LANE:ID_LANE + 1]
                pick[:, s * rows:(s + 1) * rows] = jnp.where(local == ids, 1.0, 0.0).T.astype(bf16)
        if r < 5:
            data = jnp.concatenate([got[r, :, s, :, :].reshape(rows, 128) for s in range(2)], axis=0)
        else:
            both = ggot[...].reshape(rows, 128)
            data = jnp.concatenate([jnp.where(lane < 64, both, 0.0), jnp.where(lane < 64, 0.0, both)], axis=0)
        comb[r] = doubled(pick[...], data)
        swaps[r].start()
        if r > 0:
            forward(r - 1)
    forward(5)
    for group in along:
        for copy in group:
            copy.wait_recv()
    for r in range(6):
        total = zgot[r, 0]
        for i in range(1, NZ):
            total = total + zgot[r, i]
        out[r, 8:24, :] = total
    halo = [
        remote(out.at[:, 16:24, :], out.at[:, 0:8, :], hs.at[0], hr.at[0], right),
        remote(out.at[:, 8:16, :], out.at[:, 24:32, :], hs.at[1], hr.at[1], left),
    ]
    for copy in halo:
        copy.start()
    for copy in gather_z + gather_p + gather_c + sum(terms, []) + gterms + swaps + sum(along, []):
        copy.wait_send()
    for copy in halo:
        copy.wait()


def sweep_kernel(red, steps, out, steps_out):
    steps_out[...] = steps[...]
    rank = lax.axis_index("cells") * NX + lax.axis_index("tm")
    shape = (32, 128)
    row = lax.broadcasted_iota(jnp.int32, shape, 0)
    lane = lax.broadcasted_iota(jnp.int32, shape, 1)
    k = lane % KB
    beyond = ((row == 7) & (rank == 0)) | ((row == 24) & (rank == DEV - 1))
    valid = jnp.where(beyond, 0.0, 1.0)
    ahead, behind = {}, {}
    for n in range(10):
        comp = red[n % 5]
        start = (n // 5) * 64
        for t in range(4):
            value = jnp.take_along_axis(comp, start + t * 16 + k, axis=1)
            ahead[n, t] = jnp.where(k + t < KB, value, 0.0) if t else value
            if t:
                value = jnp.take_along_axis(comp, start + t * 16 + (k + KB - t) % KB, axis=1)
                behind[n, t] = jnp.where(k >= t, value, 0.0)
    for n, (i, j) in enumerate(PAIRS):
        if i == j:
            ahead[n, 0] = ahead[n, 0] + 34.0
    fold = red[5]
    fold = fold + pltpu.roll(fold, 64, 1)
    gradient = [jnp.take_along_axis(fold, m * KB + k, axis=1) for m in range(4)]

    def pair(i, j):
        return PAIR_OF[(min(i, j), max(i, j))]

    lower, inverse = cholesky(lambda i, j: ahead[pair(i, j), 0], 4)
    x = [0.5 * v * valid for v in substitute(lower, inverse, gradient, 4)]
    for _ in range(ITERS - 1):
        misfit = list(gradient)
        for n in range(4):
            up = {t: pltpu.roll(x[n], 128 - t, 1) for t in (1, 2, 3)}
            down = {t: pltpu.roll(x[n], t, 1) for t in (1, 2, 3)}
            for m in range(4):
                p = pair(m, n)
                acc = ahead[p, 0] * x[n]
                for t in (1, 2, 3):
                    acc = acc + ahead[p, t] * up[t] + behind[p, t] * down[t]
                misfit[m] = misfit[m] - acc
            before = jnp.where(k == 0, pltpu.roll(down[1], 1, 0), down[1])
            after = jnp.where(k == KB - 1, pltpu.roll(up[1], 31, 0), up[1])
            misfit[n] = misfit[n] + 16.0 * (before + after)
        x = [(v + 0.5 * w) * valid for v, w in zip(x, substitute(lower, inverse, misfit, 4))]
    sub8 = lax.broadcasted_iota(jnp.int32, (8, 128), 0)
    keep = sub8 == lax.broadcasted_iota(jnp.int32, (8, 128), 1) // KB
    for m in range(4):
        for h in range(2):
            part = jnp.where(keep, x[m][8 + h * 8:16 + h * 8], 0.0)
            out[m:m + 1, h * 128:(h + 1) * 128] = jnp.sum(part, axis=0, keepdims=True)


def per_device(
    attitude, star_partials, attitude_partials, observed, phase, knot_offset, cell_counts, interval_owner, block_slot
):
    dma = pltpu.SemaphoreType.DMA
    owners = interval_owner.reshape(CELLS_HERE, NT)
    peers, column = NP - 1, NZ - 1
    steps, reduced = pl.pallas_call(
        main_kernel,
        out_shape=(
            jax.ShapeDtypeStruct((5, CELLS_HERE * CS), f32),
            jax.ShapeDtypeStruct((6, 32, 128), f32),
        ),
        in_specs=[SMEM, SMEM, SMEM] + [VMEM] * 6,
        out_specs=(VMEM, VMEM),
        scratch_shapes=[
            pltpu.VMEM((NZ, NY * NC * NX, 8, 128), f32),
            pltpu.VMEM((10 * TR, 128), f32),
            pltpu.VMEM((8 * TR, 128), f32),
            pltpu.VMEM((TR, 128), jnp.int32),
            pltpu.VMEM((TR, 128), jnp.int32),
            pltpu.VMEM((5 * TR, 128), f32),
            pltpu.VMEM((5, 2, DEV, 128), f32),
            pltpu.VMEM((TR * KB, 128), bf16),
            pltpu.VMEM((TR * KB, 128), bf16),
            pltpu.VMEM((4 * TR, 128), f32),
            pltpu.VMEM((TR, 128), f32),
            pltpu.VMEM((24, CELLS_HERE * CS), f32),
            pltpu.VMEM((2 * DEV, TR), bf16),
            pltpu.VMEM((QIN * KB, 2 * NP * QIN), bf16),
            pltpu.VMEM((TR, 128), f32),
            pltpu.VMEM((DEV, 128), f32),
            pltpu.VMEM((5, NP, 2, QIN, 128), f32),
            pltpu.VMEM((NP, QIN, 128), f32),
            pltpu.VMEM((6, QIN * KB, 128), f32),
            pltpu.VMEM((6, NZ * KB, 128), f32),
            pltpu.VMEM((6, NZ * KB, 128), f32),
            pltpu.VMEM((6, NZ, KB, 128), f32),
            dma((column,)), dma((column,)), dma((peers,)), dma((peers,)), dma((NY,)), dma((NY,)),
            dma((5, peers)), dma((5, peers)), dma((peers,)), dma((peers,)), dma((6,)), dma((6,)),
            dma((6, column)), dma((6, column)), dma((2,)), dma((2,)),
        ],
        compiler_params=pltpu.CompilerParams(collective_id=0, has_side_effects=True),
        name="exchange",
    )(
        cell_counts, owners, block_slot, attitude,
        star_partials, attitude_partials, observed, phase, knot_offset,
    )
    attitude_step, star_step = pl.pallas_call(
        sweep_kernel,
        out_shape=(
            jax.ShapeDtypeStruct((4, 256), f32),
            jax.ShapeDtypeStruct((5, CELLS_HERE * CS), f32),
        ),
        in_specs=[VMEM, VMEM],
        out_specs=(VMEM, VMEM),
        name="sweeps",
    )(reduced, steps)
    return (star_step, attitude_step)


def solution(mesh):
    both = ("cells", "tm")
    placed = (
        P(None, both), P(None, None, both), P(None, None, both), P(None, both), P(None, both), P(None, both),
        P(both), P(both, None, None), P(both, None),
    )
    return jax.shard_map(
        per_device, mesh=mesh, in_specs=placed, out_specs=(P(None, both), P(None, both)), check_vma=False
    )
```

```python
import functools

import jax
import jax.numpy as jnp
from jax import lax
from jax.experimental import pallas as pl
from jax.experimental.pallas import tpu as pltpu
from jax.sharding import PartitionSpec as P

NT, CS, KB, ITERS = 64, 128, 16, 6
NX, NY, NZ, NC = 4, 4, 8, 2
NP = NX * NY
DEV = NP * NZ * NC
QIN = NZ * NC
CELLS_HERE = 4
TR = CELLS_HERE * NT
ID_LANE = 63
EARLY = 1
MESH = pl.DeviceIdType.MESH
f32, bf16 = jnp.float32, jnp.bfloat16
PAIRS = [(m, n) for m in range(4) for n in range(m, 4)]
PAIR_OF = {pair: i for i, pair in enumerate(PAIRS)}
SHIFTS = [(t, i) for t in range(4) for i in range(4 - t)]
SHIFT_OF = {pair: i for i, pair in enumerate(SHIFTS)}
VMEM = pl.BlockSpec(memory_space=pltpu.VMEM)
SMEM = pl.BlockSpec(memory_space=pltpu.SMEM)


def place():
    cells, x = lax.axis_index("cells"), lax.axis_index("tm")
    z, y, c = lax.div(cells, NY * NC), lax.rem(lax.div(cells, NC), NY), lax.rem(cells, NC)
    return x, y, z, c


def device(x, y, z, c):
    return ((z * NY + y) * NC + c, x)


def remote(src, dst, send, recv, target):
    return pltpu.make_async_remote_copy(
        src_ref=src, dst_ref=dst, send_sem=send, recv_sem=recv, device_id=target, device_id_type=MESH
    )


def plane_peers(x, y, z, c):
    xs = [x] + [lax.rem(x + d, NX) for d in range(1, NX)]
    ys = [y] + [lax.rem(y + d, NY) for d in range(1, NY)]
    return [(i * NY + j, device(i, j, z, c)) for i in xs for j in ys][1:]


def column_peers(x, y, z, c):
    return [(zz, device(x, y, zz, c)) for zz in [lax.rem(z + i, NZ) for i in range(1, NZ)]]


def greet(targets):
    barrier = pltpu.get_barrier_semaphore()
    for target in targets:
        pl.semaphore_signal(barrier, inc=1, device_id=target, device_id_type=MESH)
    return lambda: pl.semaphore_wait(barrier, len(targets))


def split(value):
    high = value.astype(bf16)
    low = (value - high.astype(f32)).astype(bf16)
    return high, low


def cholesky(entries, size):
    lower = [[None] * size for _ in range(size)]
    inverse = [None] * size
    for col in range(size):
        total = entries(col, col)
        for k in range(col):
            total = total - lower[col][k] * lower[col][k]
        inverse[col] = 1.0 / jnp.sqrt(total)
        for row in range(col + 1, size):
            acc = entries(row, col)
            for k in range(col):
                acc = acc - lower[row][k] * lower[col][k]
            lower[row][col] = acc * inverse[col]
    return lower, inverse


def substitute(lower, inverse, rhs, size):
    forward = []
    for row in range(size):
        acc = rhs[row]
        for k in range(row):
            acc = acc - lower[row][k] * forward[k]
        forward.append(acc * inverse[row])
    answer = [None] * size
    for row in reversed(range(size)):
        acc = forward[row]
        for k in range(row + 1, size):
            acc = acc - lower[k][row] * answer[k]
        answer[row] = acc * inverse[row]
    return answer


def spline(t, live):
    square = t * t
    cube = square * t
    rest = 1.0 - t
    return [
        rest * rest * rest * (1.0 / 6.0) * live,
        (3.0 * cube - 6.0 * square + 4.0) * (1.0 / 6.0) * live,
        (-3.0 * cube + 3.0 * square + 3.0 * t + 1.0) * (1.0 / 6.0) * live,
        cube * (1.0 / 6.0) * live,
    ]


def spread(rows, hits):
    value = jnp.zeros((16, 128), f32)
    for row, hit in reversed(list(zip(rows, hits))):
        value = jnp.where(hit, jnp.broadcast_to(row, (16, 128)), value)
    return value


def nt_dot(left, right):
    return lax.dot_general(left, right, (((1,), (1,)), ((), ())), preferred_element_type=f32)


def aligned(value):
    return pl.multiple_of(value, 8)


def main_kernel(
    counts, owners, slots, att_in, star, axis, observed, phase, offset,
    step_ref, out,
    att, cross, parts, offs, ownm, nrm, pay, sh, sl, table, first, sums, order, pick, grads, gpay, got, ggot,
    comb, part, zsum, zgot,
    zs, zr, ps, pr, cs, cr, ns, nr, gs, gr, ws, wr, us, ur, hs, hr,
):
    x, y, z, c = place()
    plane, column = plane_peers(x, y, z, c), column_peers(x, y, z, c)
    partner = device(x, y, z, 1 - c)
    rank = ((z * NY + y) * NC + c) * NX + x
    after, before = lax.rem(rank + 1, DEV), lax.rem(rank + DEV - 1, DEV)
    right, left = [(lax.div(d, NX), lax.rem(d, NX)) for d in (after, before)]
    all_here = greet([t for _, t in plane] + [t for _, t in column] + [partner, right, left])
    here = x * NY + y
    spot = y * NX + x

    sub8 = lax.broadcasted_iota(jnp.int32, (8, 128), 0)
    lane8 = lax.broadcasted_iota(jnp.int32, (8, 128), 1)
    knot = lax.broadcasted_iota(jnp.int32, (16, 128), 0)
    att[c, z, spot, 0:4, :] = att_in[:, 0:128]
    att[c, z, spot, 4:8, :] = att_in[:, 128:256]

    for cell in range(CELLS_HERE):
        lanes = slice(cell * CS, (cell + 1) * CS)

        def prepare(g, acc, cell=cell, lanes=lanes):
            rows = pl.ds(aligned(g * 8), 8)
            at = cell * NT + g * 8
            live = jnp.where(sub8 + g * 8 < counts[cell], 1.0, 0.0)
            b = spline(phase[rows, lanes], live)
            offs[pl.ds(aligned(at), 8), :] = offset[rows, lanes]
            for n, (shift, i) in enumerate(SHIFTS):
                cross[pl.ds(aligned(n * TR + at), 8), :] = b[i] * b[i + shift]
            for m in range(4):
                parts[pl.ds(aligned(m * TR + at), 8), :] = axis[m, rows, lanes]
                parts[pl.ds(aligned((4 + m) * TR + at), 8), :] = b[m]
            for jj in range(8):
                ownm[pl.ds(at + jj, 1), :] = jnp.full((1, 128), owners[cell, g * 8 + jj], jnp.int32)
            p = [star[m, rows, lanes] * live for m in range(5)]
            terms = [p[i] * p[j] for i in range(5) for j in range(i + 1)]
            return tuple(s + term for s, term in zip(acc, terms))

        acc = lax.fori_loop(0, NT // 8, prepare, tuple(jnp.zeros((8, 128), f32) for _ in range(15)))
        for n in range(15):
            sums[n:n + 1, lanes] = jnp.sum(acc[n], axis=0, keepdims=True)

    def sides(at):
        gap = knot - jnp.broadcast_to(offs[pl.ds(at, 1), :], (16, 128))
        hits = [gap == i for i in range(4)]
        right = jnp.concatenate(
            [
                spread([cross[pl.ds(SHIFT_OF[(s, i)] * TR + at, 1), :] for i in range(4 - s)], hits)
                for s in range(4)
            ],
            axis=0,
        )
        a = [jnp.broadcast_to(parts[pl.ds(m * TR + at, 1), :], (8, 128)) for m in range(4)]
        top = jnp.where(sub8 == 4, a[1], a[0]) * jnp.where(
            sub8 == 0, a[0], jnp.where(sub8 == 2, a[2], jnp.where(sub8 == 3, a[3], a[1]))
        )
        bottom = jnp.where(sub8 < 2, a[1], jnp.where(sub8 == 4, a[3], a[2])) * jnp.where(
            (sub8 == 0) | (sub8 == 2), a[2], a[3]
        )
        rh, rl = split(right)
        lh, ll = split(jnp.concatenate([top, bottom], axis=0))
        return jnp.concatenate([lh, ll], axis=0), jnp.concatenate([rh, rl], axis=0)

    def finish(at, slot, big):
        total = big[0:16] + big[16:32]
        total = total + pltpu.roll(total, 64, 1)
        packed = jnp.where(lane8 < 64, total[0:8], total[8:16])
        packed = jnp.where((sub8 == 0) & (lane8 == ID_LANE), slot.astype(f32), packed)
        nrm[pl.ds(at, 5, stride=TR), :] = packed[0:5]

    blank = jnp.zeros((32, 128), bf16)

    def normals(g, carry):
        for jj in range(0, 32, 2):
            at = g * 32 + jj
            left0, right0 = sides(at)
            left1, right1 = sides(at + 1)
            left = jnp.concatenate(
                [jnp.concatenate([left0, blank], axis=1), jnp.concatenate([blank, left1], axis=1)], axis=0
            )
            big = nt_dot(left, jnp.concatenate([right0, right1], axis=1))
            for e in range(2):
                slot = slots[lax.shift_right_logical(g, 1), (g & 1) * 32 + jj + e]
                finish(at + e, slot, big[e * 32:(e + 1) * 32])
        return carry

    lax.fori_loop(0, 4, normals, 0)

    all_here()
    slab = att.at[c, z, spot]
    lines = att.at[c, :, spot]
    sheet = att.at[c, z]
    near = [remote(slab, slab, zs.at[i], zr.at[i], t) for i, (_, t) in enumerate(column)]
    wide = [remote(lines, lines, ps.at[i], pr.at[i], t) for i, (_, t) in enumerate(plane)]
    flat = [remote(slab, slab, ps.at[i], pr.at[i], t) for i, (_, t) in enumerate(plane)]
    deep = [remote(sheet, sheet, zs.at[i], zr.at[i], t) for i, (_, t) in enumerate(column)]

    def start_all(copies):
        for copy in copies:
            copy.start()

    def arrive(copies):
        for copy in copies:
            copy.wait_recv()

    def leave(copies):
        for copy in copies:
            copy.wait_send()

    pl.when(c == 0)(lambda: start_all(near))
    pl.when(c == 1)(lambda: start_all(flat))

    lax.fori_loop(4, 6, normals, 0)

    @pl.when(c == 1)
    def _():
        arrive(flat)
        start_all(deep)

    lax.fori_loop(6, TR // 32, normals, 0)

    owner = jnp.concatenate([ownm[...], ownm[...]], axis=1)
    other = owner.astype(f32).T
    left_of = lax.broadcasted_iota(jnp.int32, (TR, TR), 1) < lax.broadcasted_iota(jnp.int32, (TR, TR), 0)
    same = jnp.where((owner.astype(f32) == other) & left_of, 1.0, 0.0)
    place_in = jnp.sum(same, axis=1, keepdims=True).astype(jnp.int32)
    q = ((owner & 3) << 6) | ((owner & 24) << 1) | ((owner & 4) << 1) | lax.shift_right_logical(owner, 5)
    code = q + place_in * DEV
    target = lax.broadcasted_iota(jnp.int32, (TR, DEV), 1)
    for s in range(2):
        order[s * DEV:(s + 1) * DEV, :] = jnp.where(code == target + s * DEV, 1.0, 0.0).T.astype(bf16)

    @pl.when(c == 0)
    def _():
        arrive(near)
        start_all(wide)

    def doubled(matrix, data):
        big = jnp.dot(matrix, jnp.concatenate(split(data), axis=1), preferred_element_type=f32)
        return big[:, 0:128] + big[:, 128:256]

    terms = []
    for r in range(5):
        sorted_rows = doubled(order[...], nrm[r * TR:(r + 1) * TR, :])
        for s in range(2):
            pay[r, s] = sorted_rows[s * DEV:(s + 1) * DEV]
        terms.append([
            remote(pay.at[r, :, pl.ds(p * QIN, QIN), :], got.at[r, here], ns.at[r, i], nr.at[r, i], t)
            for i, (p, t) in enumerate(plane)
        ])
        if r < EARLY:
            start_all(terms[r])
    got[:, here] = pay[:, :, pl.ds(pl.multiple_of(here * QIN, QIN), QIN), :]

    def spreads(g, carry):
        pieces = []
        for jj in range(8):
            at = g * 8 + jj
            gap = knot - jnp.broadcast_to(offs[pl.ds(at, 1), :], (16, 128))
            pieces.append(spread([parts[pl.ds((4 + i) * TR + at, 1), :] for i in range(4)], [gap == i for i in range(4)]))
        high, low = split(jnp.concatenate(pieces, axis=0))
        where = pl.ds(pl.multiple_of(g * 128, 128), 128)
        sh[where, :] = high
        sl[where, :] = low
        return carry

    lax.fori_loop(0, TR // 8, spreads, 0)

    def entry(i, j):
        n = i * (i + 1) // 2 + j
        return sums[n:n + 1, :] + (1.0 if i == j else 0.0)

    lower, inverse = cholesky(entry, 5)

    pl.when(c == 0)(lambda: arrive(wide))
    pl.when(c == 1)(lambda: arrive(deep))
    whole = att.at[c]
    gather_c = remote(whole, whole, cs, cr, partner)
    gather_c.start()
    for r in range(EARLY, 5):
        start_all(terms[r])
    gather_c.wait_recv()

    lane4 = lax.broadcasted_iota(jnp.int32, (4, 128), 1) // KB

    def choose(g, carry):
        cell, base = lax.shift_right_logical(g, 3), (g & 7) * 8
        for jj in range(8):
            owner, slot = owners[cell, base + jj], slots[cell, base + jj]
            rows4 = att[
                lax.shift_right_logical(owner & 4, 2), lax.shift_right_logical(owner, 5),
                ((owner & 24) >> 1) | (owner & 3), pl.ds((slot & 8) >> 1, 4), :
            ]
            table[pl.ds(g * 32 + jj, 4, stride=8), :] = jnp.where(lane4 == (slot & 7), rows4, 0.0)
        return carry

    lax.fori_loop(0, TR // 8, choose, 0)

    lane32 = lax.broadcasted_iota(jnp.int32, (32, 128), 1)
    row32 = lax.broadcasted_iota(jnp.int32, (32, 128), 0)
    own = (lane32 // KB) == (row32 % 8)

    def fold(value):
        for shift in (64, 32, 16):
            value = value + pltpu.roll(value, shift, 1)
        return value

    for cell in range(CELLS_HERE):
        lanes = slice(cell * CS, (cell + 1) * CS)

        def predict(g, acc, cell=cell, lanes=lanes):
            rows = pl.ds(aligned(g * 8), 8)
            gg = cell * 8 + g
            live = jnp.where(sub8 + g * 8 < counts[cell], 1.0, 0.0)
            coeff = jnp.where(own, fold(table[pl.ds(aligned(gg * 32), 32), :]), 0.0)
            high, low = split(coeff)
            where = pl.ds(pl.multiple_of(gg * 128, 128), 128)
            big = jnp.dot(jnp.concatenate([high, low], axis=0), sh[where, :], preferred_element_type=f32)
            fit = big[0:32] + big[32:64] + jnp.dot(high, sl[where, :], preferred_element_type=f32)
            value = live * observed[rows, lanes]
            for m in range(4):
                value = value - axis[m, rows, lanes] * fit[m * 8:(m + 1) * 8]
            first[pl.ds(aligned(gg * 8), 8), :] = value
            return tuple(s + star[n, rows, lanes] * value for n, s in enumerate(acc))

        acc = lax.fori_loop(0, NT // 8, predict, tuple(jnp.zeros((8, 128), f32) for _ in range(5)), unroll=4)
        for n in range(5):
            sums[15 + n:16 + n, lanes] = jnp.sum(acc[n], axis=0, keepdims=True)

    steps = substitute(lower, inverse, [sums[15 + n:16 + n, :] for n in range(5)], 5)
    for n in range(5):
        step_ref[n:n + 1, :] = steps[n]

    for cell in range(CELLS_HERE):
        lanes = slice(cell * CS, (cell + 1) * CS)

        def gradients(g, carry, cell=cell, lanes=lanes):
            rows = pl.ds(aligned(g * 8), 8)
            gg = cell * 8 + g
            live = jnp.where(sub8 + g * 8 < counts[cell], 1.0, 0.0)
            fitted = star[0, rows, lanes] * step_ref[0:1, lanes]
            for n in range(1, 5):
                fitted = fitted + star[n, rows, lanes] * step_ref[n:n + 1, lanes]
            second = first[pl.ds(aligned(gg * 8), 8), :] - live * fitted
            high, low = split(jnp.concatenate([axis[m, rows, lanes] * second for m in range(4)], axis=0))
            where = pl.ds(pl.multiple_of(gg * 128, 128), 128)
            big = nt_dot(jnp.concatenate([high, low], axis=0), sh[where, :])
            total = big[0:32] + big[32:64] + nt_dot(high, sl[where, :])
            total = fold(jnp.where(own, total, 0.0))
            grad = jnp.zeros((8, 128), f32)
            for m in range(4):
                grad = jnp.where((lane8 // KB) % 4 == m, total[m * 8:(m + 1) * 8], grad)
            grads[pl.ds(aligned(gg * 8), 8), :] = grad
            return carry

        lax.fori_loop(0, NT // 8, gradients, 0, unroll=4)

    lane = lax.broadcasted_iota(jnp.int32, (TR, 128), 1)
    placed = doubled(order[...], grads[...])
    gpay[...] = jnp.where(lane < 64, placed[0:DEV], placed[DEV:2 * DEV])
    gterms = [
        remote(gpay.at[pl.ds(p * QIN, QIN), :], ggot.at[here], gs.at[i], gr.at[i], t) for i, (p, t) in enumerate(plane)
    ]
    for copy in gterms:
        copy.start()
    ggot[here] = gpay[pl.ds(pl.multiple_of(here * QIN, QIN), QIN), :]

    rows = NP * QIN
    cols = QIN * KB
    half = NZ * KB
    keep = pl.ds(pl.multiple_of(c * half, half), half)
    give = pl.ds(pl.multiple_of((1 - c) * half, half), half)
    swaps = [remote(comb.at[r, give, :], part.at[r], ws.at[r], wr.at[r], partner) for r in range(6)]
    along = [
        [
            remote(zsum.at[r, pl.ds(zz * KB, KB), :], zgot.at[r, z], us.at[r, i], ur.at[r, i], t)
            for i, (zz, t) in enumerate(column)
        ]
        for r in range(6)
    ]

    def forward(r):
        swaps[r].wait_recv()
        zsum[r] = comb[r, keep, :] + part[r]
        for copy in along[r]:
            copy.start()
        zgot[r, z] = zsum[r, pl.ds(pl.multiple_of(z * KB, KB), KB), :]

    for r in range(6):
        for copy in terms[r] if r < 5 else gterms:
            copy.wait_recv()
        if r == 0:
            row = lax.broadcasted_iota(jnp.int32, (rows, cols), 0)
            col = lax.broadcasted_iota(jnp.int32, (rows, cols), 1)
            local = (col - (row % QIN) * KB).astype(f32)
            for s in range(2):
                ids = got[0, :, s, :, :].reshape(rows, 128)[:, ID_LANE:ID_LANE + 1]
                pick[:, s * rows:(s + 1) * rows] = jnp.where(local == ids, 1.0, 0.0).T.astype(bf16)
        if r < 5:
            data = jnp.concatenate([got[r, :, s, :, :].reshape(rows, 128) for s in range(2)], axis=0)
        else:
            both = ggot[...].reshape(rows, 128)
            data = jnp.concatenate([jnp.where(lane < 64, both, 0.0), jnp.where(lane < 64, 0.0, both)], axis=0)
        comb[r] = doubled(pick[...], data)
        swaps[r].start()
        if r > 0:
            forward(r - 1)
    forward(5)
    for group in along:
        for copy in group:
            copy.wait_recv()
    for r in range(6):
        total = zgot[r, 0]
        for i in range(1, NZ):
            total = total + zgot[r, i]
        out[r, 8:24, :] = total
    halo = [
        remote(out.at[:, 16:24, :], out.at[:, 0:8, :], hs.at[0], hr.at[0], right),
        remote(out.at[:, 8:16, :], out.at[:, 24:32, :], hs.at[1], hr.at[1], left),
    ]
    for copy in halo:
        copy.start()
    pl.when(c == 0)(lambda: leave(near + wide))
    pl.when(c == 1)(lambda: leave(flat + deep))
    leave([gather_c] + sum(terms, []) + gterms + swaps + sum(along, []))
    for copy in halo:
        copy.wait()


def sweep_kernel(red, steps, out, steps_out):
    steps_out[...] = steps[...]
    rank = lax.axis_index("cells") * NX + lax.axis_index("tm")
    shape = (32, 128)
    row = lax.broadcasted_iota(jnp.int32, shape, 0)
    lane = lax.broadcasted_iota(jnp.int32, shape, 1)
    k = lane % KB
    beyond = ((row == 7) & (rank == 0)) | ((row == 24) & (rank == DEV - 1))
    valid = jnp.where(beyond, 0.0, 1.0)
    ahead, behind = {}, {}
    for n in range(10):
        comp = red[n % 5]
        start = (n // 5) * 64
        for t in range(4):
            value = jnp.take_along_axis(comp, start + t * 16 + k, axis=1)
            ahead[n, t] = jnp.where(k + t < KB, value, 0.0) if t else value
            if t:
                value = jnp.take_along_axis(comp, start + t * 16 + (k + KB - t) % KB, axis=1)
                behind[n, t] = jnp.where(k >= t, value, 0.0)
    for n, (i, j) in enumerate(PAIRS):
        if i == j:
            ahead[n, 0] = ahead[n, 0] + 34.0
    fold = red[5]
    fold = fold + pltpu.roll(fold, 64, 1)
    gradient = [jnp.take_along_axis(fold, m * KB + k, axis=1) for m in range(4)]

    def pair(i, j):
        return PAIR_OF[(min(i, j), max(i, j))]

    lower, inverse = cholesky(lambda i, j: ahead[pair(i, j), 0], 4)
    x = [0.5 * v * valid for v in substitute(lower, inverse, gradient, 4)]
    for _ in range(ITERS - 1):
        misfit = list(gradient)
        for n in range(4):
            up = {t: pltpu.roll(x[n], 128 - t, 1) for t in (1, 2, 3)}
            down = {t: pltpu.roll(x[n], t, 1) for t in (1, 2, 3)}
            for m in range(4):
                p = pair(m, n)
                acc = ahead[p, 0] * x[n]
                for t in (1, 2, 3):
                    acc = acc + ahead[p, t] * up[t] + behind[p, t] * down[t]
                misfit[m] = misfit[m] - acc
            before = jnp.where(k == 0, pltpu.roll(down[1], 1, 0), down[1])
            after = jnp.where(k == KB - 1, pltpu.roll(up[1], 31, 0), up[1])
            misfit[n] = misfit[n] + 16.0 * (before + after)
        x = [(v + 0.5 * w) * valid for v, w in zip(x, substitute(lower, inverse, misfit, 4))]
    sub8 = lax.broadcasted_iota(jnp.int32, (8, 128), 0)
    keep = sub8 == lax.broadcasted_iota(jnp.int32, (8, 128), 1) // KB
    for m in range(4):
        for h in range(2):
            part = jnp.where(keep, x[m][8 + h * 8:16 + h * 8], 0.0)
            out[m:m + 1, h * 128:(h + 1) * 128] = jnp.sum(part, axis=0, keepdims=True)


def per_device(
    attitude, star_partials, attitude_partials, observed, phase, knot_offset, cell_counts, interval_owner, block_slot
):
    dma = pltpu.SemaphoreType.DMA
    owners = interval_owner.reshape(CELLS_HERE, NT)
    peers, column = NP - 1, NZ - 1
    steps, reduced = pl.pallas_call(
        main_kernel,
        out_shape=(
            jax.ShapeDtypeStruct((5, CELLS_HERE * CS), f32),
            jax.ShapeDtypeStruct((6, 32, 128), f32),
        ),
        in_specs=[SMEM, SMEM, SMEM] + [VMEM] * 6,
        out_specs=(VMEM, VMEM),
        scratch_shapes=[
            pltpu.VMEM((NC, NZ, NY * NX, 8, 128), f32),
            pltpu.VMEM((10 * TR, 128), f32),
            pltpu.VMEM((8 * TR, 128), f32),
            pltpu.VMEM((TR, 128), jnp.int32),
            pltpu.VMEM((TR, 128), jnp.int32),
            pltpu.VMEM((5 * TR, 128), f32),
            pltpu.VMEM((5, 2, DEV, 128), f32),
            pltpu.VMEM((TR * KB, 128), bf16),
            pltpu.VMEM((TR * KB, 128), bf16),
            pltpu.VMEM((4 * TR, 128), f32),
            pltpu.VMEM((TR, 128), f32),
            pltpu.VMEM((24, CELLS_HERE * CS), f32),
            pltpu.VMEM((2 * DEV, TR), bf16),
            pltpu.VMEM((QIN * KB, 2 * NP * QIN), bf16),
            pltpu.VMEM((TR, 128), f32),
            pltpu.VMEM((DEV, 128), f32),
            pltpu.VMEM((5, NP, 2, QIN, 128), f32),
            pltpu.VMEM((NP, QIN, 128), f32),
            pltpu.VMEM((6, QIN * KB, 128), f32),
            pltpu.VMEM((6, NZ * KB, 128), f32),
            pltpu.VMEM((6, NZ * KB, 128), f32),
            pltpu.VMEM((6, NZ, KB, 128), f32),
            dma((column,)), dma((column,)), dma((peers,)), dma((peers,)), dma, dma,
            dma((5, peers)), dma((5, peers)), dma((peers,)), dma((peers,)), dma((6,)), dma((6,)),
            dma((6, column)), dma((6, column)), dma((2,)), dma((2,)),
        ],
        compiler_params=pltpu.CompilerParams(collective_id=0, has_side_effects=True),
        name="exchange",
    )(
        cell_counts, owners, block_slot, attitude,
        star_partials, attitude_partials, observed, phase, knot_offset,
    )
    attitude_step, star_step = pl.pallas_call(
        sweep_kernel,
        out_shape=(
            jax.ShapeDtypeStruct((4, 256), f32),
            jax.ShapeDtypeStruct((5, CELLS_HERE * CS), f32),
        ),
        in_specs=[VMEM, VMEM],
        out_specs=(VMEM, VMEM),
        name="sweeps",
    )(reduced, steps)
    return (star_step, attitude_step)


def solution(mesh):
    both = ("cells", "tm")
    placed = (
        P(None, both), P(None, None, both), P(None, None, both), P(None, both), P(None, both), P(None, both),
        P(both), P(both, None, None), P(both, None),
    )
    return jax.shard_map(
        per_device, mesh=mesh, in_specs=placed, out_specs=(P(None, both), P(None, both)), check_vma=False
    )
```

```python
import functools

import jax
import jax.numpy as jnp
from jax import lax
from jax.experimental import pallas as pl
from jax.experimental.pallas import tpu as pltpu
from jax.sharding import PartitionSpec as P

NT, CS, KB, ITERS = 64, 128, 16, 6
NX, NY, NZ, NC = 4, 4, 8, 2
NP = NX * NY
DEV = NP * NZ * NC
QIN = NZ * NC
CELLS_HERE = 4
TR = CELLS_HERE * NT
ID_LANE = 63
EARLY = 2
MESH = pl.DeviceIdType.MESH
f32, bf16 = jnp.float32, jnp.bfloat16
PAIRS = [(m, n) for m in range(4) for n in range(m, 4)]
PAIR_OF = {pair: i for i, pair in enumerate(PAIRS)}
SHIFTS = [(t, i) for t in range(4) for i in range(4 - t)]
SHIFT_OF = {pair: i for i, pair in enumerate(SHIFTS)}
VMEM = pl.BlockSpec(memory_space=pltpu.VMEM)
SMEM = pl.BlockSpec(memory_space=pltpu.SMEM)


def place():
    cells, x = lax.axis_index("cells"), lax.axis_index("tm")
    z, y, c = lax.div(cells, NY * NC), lax.rem(lax.div(cells, NC), NY), lax.rem(cells, NC)
    return x, y, z, c


def device(x, y, z, c):
    return ((z * NY + y) * NC + c, x)


def remote(src, dst, send, recv, target):
    return pltpu.make_async_remote_copy(
        src_ref=src, dst_ref=dst, send_sem=send, recv_sem=recv, device_id=target, device_id_type=MESH
    )


def plane_peers(x, y, z, c):
    xs = [x] + [lax.rem(x + d, NX) for d in range(1, NX)]
    ys = [y] + [lax.rem(y + d, NY) for d in range(1, NY)]
    return [(i * NY + j, device(i, j, z, c)) for i in xs for j in ys][1:]


def column_peers(x, y, z, c):
    return [(zz, device(x, y, zz, c)) for zz in [lax.rem(z + i, NZ) for i in range(1, NZ)]]


def greet(targets):
    barrier = pltpu.get_barrier_semaphore()
    for target in targets:
        pl.semaphore_signal(barrier, inc=1, device_id=target, device_id_type=MESH)
    return lambda: pl.semaphore_wait(barrier, len(targets))


def split(value):
    high = value.astype(bf16)
    low = (value - high.astype(f32)).astype(bf16)
    return high, low


def cholesky(entries, size):
    lower = [[None] * size for _ in range(size)]
    inverse = [None] * size
    for col in range(size):
        total = entries(col, col)
        for k in range(col):
            total = total - lower[col][k] * lower[col][k]
        inverse[col] = 1.0 / jnp.sqrt(total)
        for row in range(col + 1, size):
            acc = entries(row, col)
            for k in range(col):
                acc = acc - lower[row][k] * lower[col][k]
            lower[row][col] = acc * inverse[col]
    return lower, inverse


def substitute(lower, inverse, rhs, size):
    forward = []
    for row in range(size):
        acc = rhs[row]
        for k in range(row):
            acc = acc - lower[row][k] * forward[k]
        forward.append(acc * inverse[row])
    answer = [None] * size
    for row in reversed(range(size)):
        acc = forward[row]
        for k in range(row + 1, size):
            acc = acc - lower[k][row] * answer[k]
        answer[row] = acc * inverse[row]
    return answer


def spline(t, live):
    square = t * t
    cube = square * t
    rest = 1.0 - t
    return [
        rest * rest * rest * (1.0 / 6.0) * live,
        (3.0 * cube - 6.0 * square + 4.0) * (1.0 / 6.0) * live,
        (-3.0 * cube + 3.0 * square + 3.0 * t + 1.0) * (1.0 / 6.0) * live,
        cube * (1.0 / 6.0) * live,
    ]


def spread(rows, hits):
    value = jnp.zeros((16, 128), f32)
    for row, hit in reversed(list(zip(rows, hits))):
        value = jnp.where(hit, jnp.broadcast_to(row, (16, 128)), value)
    return value


def nt_dot(left, right):
    return lax.dot_general(left, right, (((1,), (1,)), ((), ())), preferred_element_type=f32)


def aligned(value):
    return pl.multiple_of(value, 8)


def main_kernel(
    counts, owners, slots, att_in, star, axis, observed, phase, offset,
    step_ref, out,
    att, found, cross, parts, offs, ownm, nrm, pay, sh, sl, table, first, sums, order, pick, grads, gpay, got, ggot,
    comb, part, zsum, zgot,
    zs, zr, ps, pr, cs, cr, ns, nr, gs, gr, ws, wr, us, ur, hs, hr,
):
    x, y, z, c = place()
    plane, column = plane_peers(x, y, z, c), column_peers(x, y, z, c)
    partner = device(x, y, z, 1 - c)
    rank = ((z * NY + y) * NC + c) * NX + x
    after, before = lax.rem(rank + 1, DEV), lax.rem(rank + DEV - 1, DEV)
    right, left = [(lax.div(d, NX), lax.rem(d, NX)) for d in (after, before)]
    all_here = greet([t for _, t in plane] + [t for _, t in column] + [partner, right, left])
    here = x * NY + y
    spot = y * NX + x

    sub8 = lax.broadcasted_iota(jnp.int32, (8, 128), 0)
    lane8 = lax.broadcasted_iota(jnp.int32, (8, 128), 1)
    knot = lax.broadcasted_iota(jnp.int32, (16, 128), 0)
    att[c * NZ + z, spot, 0:4, :] = att_in[:, 0:128]
    att[c * NZ + z, spot, 4:8, :] = att_in[:, 128:256]

    for cell in range(CELLS_HERE):
        lanes = slice(cell * CS, (cell + 1) * CS)

        def prepare(g, acc, cell=cell, lanes=lanes):
            rows = pl.ds(aligned(g * 8), 8)
            at = cell * NT + g * 8
            live = jnp.where(sub8 + g * 8 < counts[cell], 1.0, 0.0)
            b = spline(phase[rows, lanes], live)
            offs[pl.ds(aligned(at), 8), :] = offset[rows, lanes]
            for n, (shift, i) in enumerate(SHIFTS):
                cross[pl.ds(aligned(n * TR + at), 8), :] = b[i] * b[i + shift]
            for m in range(4):
                parts[pl.ds(aligned(m * TR + at), 8), :] = axis[m, rows, lanes]
                parts[pl.ds(aligned((4 + m) * TR + at), 8), :] = b[m]
            for jj in range(8):
                ownm[pl.ds(at + jj, 1), :] = jnp.full((1, 128), owners[cell, g * 8 + jj], jnp.int32)
            p = [star[m, rows, lanes] * live for m in range(5)]
            terms = [p[i] * p[j] for i in range(5) for j in range(i + 1)]
            return tuple(s + term for s, term in zip(acc, terms))

        acc = lax.fori_loop(0, NT // 8, prepare, tuple(jnp.zeros((8, 128), f32) for _ in range(15)))
        for n in range(15):
            sums[n:n + 1, lanes] = jnp.sum(acc[n], axis=0, keepdims=True)

    def sides(at):
        gap = knot - jnp.broadcast_to(offs[pl.ds(at, 1), :], (16, 128))
        hits = [gap == i for i in range(4)]
        right = jnp.concatenate(
            [
                spread([cross[pl.ds(SHIFT_OF[(s, i)] * TR + at, 1), :] for i in range(4 - s)], hits)
                for s in range(4)
            ],
            axis=0,
        )
        a = [jnp.broadcast_to(parts[pl.ds(m * TR + at, 1), :], (8, 128)) for m in range(4)]
        top = jnp.where(sub8 == 4, a[1], a[0]) * jnp.where(
            sub8 == 0, a[0], jnp.where(sub8 == 2, a[2], jnp.where(sub8 == 3, a[3], a[1]))
        )
        bottom = jnp.where(sub8 < 2, a[1], jnp.where(sub8 == 4, a[3], a[2])) * jnp.where(
            (sub8 == 0) | (sub8 == 2), a[2], a[3]
        )
        rh, rl = split(right)
        lh, ll = split(jnp.concatenate([top, bottom], axis=0))
        return jnp.concatenate([lh, ll], axis=0), jnp.concatenate([rh, rl], axis=0)

    def finish(at, slot, big):
        total = big[0:16] + big[16:32]
        total = total + pltpu.roll(total, 64, 1)
        packed = jnp.where(lane8 < 64, total[0:8], total[8:16])
        packed = jnp.where((sub8 == 0) & (lane8 == ID_LANE), slot.astype(f32), packed)
        nrm[pl.ds(at, 5, stride=TR), :] = packed[0:5]

    blank = jnp.zeros((32, 128), bf16)

    def normals(g, carry):
        for jj in range(0, 32, 2):
            at = g * 32 + jj
            left0, right0 = sides(at)
            left1, right1 = sides(at + 1)
            left = jnp.concatenate(
                [jnp.concatenate([left0, blank], axis=1), jnp.concatenate([blank, left1], axis=1)], axis=0
            )
            big = nt_dot(left, jnp.concatenate([right0, right1], axis=1))
            for e in range(2):
                slot = slots[lax.shift_right_logical(g, 1), (g & 1) * 32 + jj + e]
                finish(at + e, slot, big[e * 32:(e + 1) * 32])
                owner = owners[lax.shift_right_logical(g, 1), (g & 1) * 32 + jj + e]
                found[0, at + e] = ((owner & 4) << 1) | lax.shift_right_logical(owner, 5)
                found[1, at + e] = lax.shift_right_logical(owner & 24, 1) | (owner & 3)
                found[2, at + e] = lax.shift_right_logical(slot & 8, 1)
                found[3, at + e] = slot & 7
        return carry

    lax.fori_loop(0, 4, normals, 0)

    all_here()
    slab = att.at[c * NZ + z, spot]
    lines = att.at[pl.ds(c * NZ, NZ), spot]
    sheet = att.at[c * NZ + z]
    near = [remote(slab, slab, zs.at[i], zr.at[i], t) for i, (_, t) in enumerate(column)]
    wide = [remote(lines, lines, ps.at[i], pr.at[i], t) for i, (_, t) in enumerate(plane)]
    flat = [remote(slab, slab, ps.at[i], pr.at[i], t) for i, (_, t) in enumerate(plane)]
    deep = [remote(sheet, sheet, zs.at[i], zr.at[i], t) for i, (_, t) in enumerate(column)]

    def start_all(copies):
        for copy in copies:
            copy.start()

    def arrive(copies):
        for copy in copies:
            copy.wait_recv()

    def leave(copies):
        for copy in copies:
            copy.wait_send()

    pl.when(c == 0)(lambda: start_all(near))
    pl.when(c == 1)(lambda: start_all(flat))

    lax.fori_loop(4, 6, normals, 0)

    @pl.when(c == 1)
    def _():
        arrive(flat)
        start_all(deep)

    lax.fori_loop(6, TR // 32, normals, 0)

    owner = jnp.concatenate([ownm[...], ownm[...]], axis=1)
    other = owner.astype(f32).T
    left_of = lax.broadcasted_iota(jnp.int32, (TR, TR), 1) < lax.broadcasted_iota(jnp.int32, (TR, TR), 0)
    same = jnp.where((owner.astype(f32) == other) & left_of, 1.0, 0.0)
    place_in = jnp.sum(same, axis=1, keepdims=True).astype(jnp.int32)
    q = ((owner & 3) << 6) | ((owner & 24) << 1) | ((owner & 4) << 1) | lax.shift_right_logical(owner, 5)
    code = q + place_in * DEV
    target = lax.broadcasted_iota(jnp.int32, (TR, DEV), 1)
    for s in range(2):
        order[s * DEV:(s + 1) * DEV, :] = jnp.where(code == target + s * DEV, 1.0, 0.0).T.astype(bf16)

    @pl.when(c == 0)
    def _():
        arrive(near)
        start_all(wide)

    def doubled(matrix, data):
        big = jnp.dot(matrix, jnp.concatenate(split(data), axis=1), preferred_element_type=f32)
        return big[:, 0:128] + big[:, 128:256]

    terms = []
    for r in range(5):
        sorted_rows = doubled(order[...], nrm[r * TR:(r + 1) * TR, :])
        for s in range(2):
            pay[r, s] = sorted_rows[s * DEV:(s + 1) * DEV]
        terms.append([
            remote(pay.at[r, :, pl.ds(p * QIN, QIN), :], got.at[r, here], ns.at[r, i], nr.at[r, i], t)
            for i, (p, t) in enumerate(plane)
        ])
        if r < EARLY:
            start_all(terms[r])
    got[:, here] = pay[:, :, pl.ds(pl.multiple_of(here * QIN, QIN), QIN), :]

    def spreads(g, carry):
        pieces = []
        for jj in range(8):
            at = g * 8 + jj
            gap = knot - jnp.broadcast_to(offs[pl.ds(at, 1), :], (16, 128))
            pieces.append(spread([parts[pl.ds((4 + i) * TR + at, 1), :] for i in range(4)], [gap == i for i in range(4)]))
        high, low = split(jnp.concatenate(pieces, axis=0))
        where = pl.ds(pl.multiple_of(g * 128, 128), 128)
        sh[where, :] = high
        sl[where, :] = low
        return carry

    lax.fori_loop(0, TR // 8, spreads, 0)

    def entry(i, j):
        n = i * (i + 1) // 2 + j
        return sums[n:n + 1, :] + (1.0 if i == j else 0.0)

    lower, inverse = cholesky(entry, 5)

    pl.when(c == 0)(lambda: arrive(wide))
    pl.when(c == 1)(lambda: arrive(deep))
    whole = att.at[pl.ds(c * NZ, NZ)]
    gather_c = remote(whole, whole, cs, cr, partner)
    gather_c.start()
    for r in range(EARLY, 5):
        start_all(terms[r])
    gather_c.wait_recv()

    lane4 = lax.broadcasted_iota(jnp.int32, (4, 128), 1) // KB

    def choose(g, carry):
        for jj in range(8):
            at = g * 8 + jj
            rows4 = att[found[0, at], found[1, at], pl.ds(found[2, at], 4), :]
            table[pl.ds(g * 32 + jj, 4, stride=8), :] = jnp.where(lane4 == found[3, at], rows4, 0.0)
        return carry

    lax.fori_loop(0, TR // 8, choose, 0)

    lane32 = lax.broadcasted_iota(jnp.int32, (32, 128), 1)
    row32 = lax.broadcasted_iota(jnp.int32, (32, 128), 0)
    own = (lane32 // KB) == (row32 % 8)

    def fold(value):
        for shift in (64, 32, 16):
            value = value + pltpu.roll(value, shift, 1)
        return value

    for cell in range(CELLS_HERE):
        lanes = slice(cell * CS, (cell + 1) * CS)

        def predict(g, acc, cell=cell, lanes=lanes):
            rows = pl.ds(aligned(g * 8), 8)
            gg = cell * 8 + g
            live = jnp.where(sub8 + g * 8 < counts[cell], 1.0, 0.0)
            coeff = jnp.where(own, fold(table[pl.ds(aligned(gg * 32), 32), :]), 0.0)
            high, low = split(coeff)
            where = pl.ds(pl.multiple_of(gg * 128, 128), 128)
            big = jnp.dot(jnp.concatenate([high, low], axis=0), sh[where, :], preferred_element_type=f32)
            fit = big[0:32] + big[32:64] + jnp.dot(high, sl[where, :], preferred_element_type=f32)
            value = live * observed[rows, lanes]
            for m in range(4):
                value = value - axis[m, rows, lanes] * fit[m * 8:(m + 1) * 8]
            first[pl.ds(aligned(gg * 8), 8), :] = value
            return tuple(s + star[n, rows, lanes] * value for n, s in enumerate(acc))

        acc = lax.fori_loop(0, NT // 8, predict, tuple(jnp.zeros((8, 128), f32) for _ in range(5)), unroll=8)
        for n in range(5):
            sums[15 + n:16 + n, lanes] = jnp.sum(acc[n], axis=0, keepdims=True)

    steps = substitute(lower, inverse, [sums[15 + n:16 + n, :] for n in range(5)], 5)
    for n in range(5):
        step_ref[n:n + 1, :] = steps[n]

    for cell in range(CELLS_HERE):
        lanes = slice(cell * CS, (cell + 1) * CS)

        def gradients(g, carry, cell=cell, lanes=lanes):
            rows = pl.ds(aligned(g * 8), 8)
            gg = cell * 8 + g
            live = jnp.where(sub8 + g * 8 < counts[cell], 1.0, 0.0)
            fitted = star[0, rows, lanes] * step_ref[0:1, lanes]
            for n in range(1, 5):
                fitted = fitted + star[n, rows, lanes] * step_ref[n:n + 1, lanes]
            second = first[pl.ds(aligned(gg * 8), 8), :] - live * fitted
            high, low = split(jnp.concatenate([axis[m, rows, lanes] * second for m in range(4)], axis=0))
            where = pl.ds(pl.multiple_of(gg * 128, 128), 128)
            big = nt_dot(jnp.concatenate([high, low], axis=0), sh[where, :])
            total = big[0:32] + big[32:64] + nt_dot(high, sl[where, :])
            total = fold(jnp.where(own, total, 0.0))
            grad = jnp.zeros((8, 128), f32)
            for m in range(4):
                grad = jnp.where((lane8 // KB) % 4 == m, total[m * 8:(m + 1) * 8], grad)
            grads[pl.ds(aligned(gg * 8), 8), :] = grad
            return carry

        lax.fori_loop(0, NT // 8, gradients, 0, unroll=8)

    lane = lax.broadcasted_iota(jnp.int32, (TR, 128), 1)
    placed = doubled(order[...], grads[...])
    gpay[...] = jnp.where(lane < 64, placed[0:DEV], placed[DEV:2 * DEV])
    gterms = [
        remote(gpay.at[pl.ds(p * QIN, QIN), :], ggot.at[here], gs.at[i], gr.at[i], t) for i, (p, t) in enumerate(plane)
    ]
    for copy in gterms:
        copy.start()
    ggot[here] = gpay[pl.ds(pl.multiple_of(here * QIN, QIN), QIN), :]

    rows = NP * QIN
    cols = QIN * KB
    half = NZ * KB
    keep = pl.ds(pl.multiple_of(c * half, half), half)
    give = pl.ds(pl.multiple_of((1 - c) * half, half), half)
    swaps = [remote(comb.at[r, give, :], part.at[r], ws.at[r], wr.at[r], partner) for r in range(6)]
    along = [
        [
            remote(zsum.at[r, pl.ds(zz * KB, KB), :], zgot.at[r, z], us.at[r, i], ur.at[r, i], t)
            for i, (zz, t) in enumerate(column)
        ]
        for r in range(6)
    ]

    def forward(r):
        swaps[r].wait_recv()
        zsum[r] = comb[r, keep, :] + part[r]
        for copy in along[r]:
            copy.start()
        zgot[r, z] = zsum[r, pl.ds(pl.multiple_of(z * KB, KB), KB), :]

    for r in range(6):
        for copy in terms[r] if r < 5 else gterms:
            copy.wait_recv()
        if r == 0:
            row = lax.broadcasted_iota(jnp.int32, (rows, cols), 0)
            col = lax.broadcasted_iota(jnp.int32, (rows, cols), 1)
            local = (col - (row % QIN) * KB).astype(f32)
            for s in range(2):
                ids = got[0, :, s, :, :].reshape(rows, 128)[:, ID_LANE:ID_LANE + 1]
                pick[:, s * rows:(s + 1) * rows] = jnp.where(local == ids, 1.0, 0.0).T.astype(bf16)
        if r < 5:
            data = jnp.concatenate([got[r, :, s, :, :].reshape(rows, 128) for s in range(2)], axis=0)
        else:
            both = ggot[...].reshape(rows, 128)
            data = jnp.concatenate([jnp.where(lane < 64, both, 0.0), jnp.where(lane < 64, 0.0, both)], axis=0)
        comb[r] = doubled(pick[...], data)
        swaps[r].start()
        if r > 0:
            forward(r - 1)
    forward(5)
    for group in along:
        for copy in group:
            copy.wait_recv()
    for r in range(6):
        total = zgot[r, 0]
        for i in range(1, NZ):
            total = total + zgot[r, i]
        out[r, 8:24, :] = total
    halo = [
        remote(out.at[:, 16:24, :], out.at[:, 0:8, :], hs.at[0], hr.at[0], right),
        remote(out.at[:, 8:16, :], out.at[:, 24:32, :], hs.at[1], hr.at[1], left),
    ]
    for copy in halo:
        copy.start()
    pl.when(c == 0)(lambda: leave(near + wide))
    pl.when(c == 1)(lambda: leave(flat + deep))
    leave([gather_c] + sum(terms, []) + gterms + swaps + sum(along, []))
    for copy in halo:
        copy.wait()


def sweep_kernel(red, steps, out, steps_out):
    steps_out[...] = steps[...]
    rank = lax.axis_index("cells") * NX + lax.axis_index("tm")
    shape = (24, 128)
    row = lax.broadcasted_iota(jnp.int32, shape, 0)
    lane = lax.broadcasted_iota(jnp.int32, shape, 1)
    k = lane % KB
    beyond = ((row == 23) & (rank == 0)) | ((row == 16) & (rank == DEV - 1))
    valid = jnp.where(beyond, 0.0, 1.0)
    last = lax.broadcasted_iota(jnp.int32, (8, 128), 0) == 7

    def loaded(r):
        return jnp.concatenate([red[r, 8:24], jnp.where(last, red[r, 0:8], red[r, 24:32])], axis=0)

    comps = [loaded(r) for r in range(6)]
    ahead, behind = {}, {}
    for n in range(10):
        comp = comps[n % 5]
        start = (n // 5) * 64
        for t in range(4):
            value = jnp.take_along_axis(comp, start + t * 16 + k, axis=1)
            ahead[n, t] = jnp.where(k + t < KB, value, 0.0) if t else value
            if t:
                value = jnp.take_along_axis(comp, start + t * 16 + (k + KB - t) % KB, axis=1)
                behind[n, t] = jnp.where(k >= t, value, 0.0)
    for n, (i, j) in enumerate(PAIRS):
        if i == j:
            ahead[n, 0] = ahead[n, 0] + 34.0
    fold = comps[5]
    fold = fold + pltpu.roll(fold, 64, 1)
    gradient = [jnp.take_along_axis(fold, m * KB + k, axis=1) for m in range(4)]

    def pair(i, j):
        return PAIR_OF[(min(i, j), max(i, j))]

    lower, inverse = cholesky(lambda i, j: ahead[pair(i, j), 0], 4)
    x = [0.5 * v * valid for v in substitute(lower, inverse, gradient, 4)]
    for _ in range(ITERS - 1):
        misfit = list(gradient)
        for n in range(4):
            up = {t: pltpu.roll(x[n], 128 - t, 1) for t in (1, 2, 3)}
            down = {t: pltpu.roll(x[n], t, 1) for t in (1, 2, 3)}
            for m in range(4):
                p = pair(m, n)
                acc = ahead[p, 0] * x[n]
                for t in (1, 2, 3):
                    acc = acc + ahead[p, t] * up[t] + behind[p, t] * down[t]
                misfit[m] = misfit[m] - acc
            before = jnp.where(k == 0, pltpu.roll(down[1], 1, 0), down[1])
            after = jnp.where(k == KB - 1, pltpu.roll(up[1], 23, 0), up[1])
            misfit[n] = misfit[n] + 16.0 * (before + after)
        x = [(v + 0.5 * w) * valid for v, w in zip(x, substitute(lower, inverse, misfit, 4))]
    sub8 = lax.broadcasted_iota(jnp.int32, (8, 128), 0)
    keep = sub8 == lax.broadcasted_iota(jnp.int32, (8, 128), 1) // KB
    for m in range(4):
        for h in range(2):
            part = jnp.where(keep, x[m][h * 8:8 + h * 8], 0.0)
            out[m:m + 1, h * 128:(h + 1) * 128] = jnp.sum(part, axis=0, keepdims=True)


def per_device(
    attitude, star_partials, attitude_partials, observed, phase, knot_offset, cell_counts, interval_owner, block_slot
):
    dma = pltpu.SemaphoreType.DMA
    owners = interval_owner.reshape(CELLS_HERE, NT)
    peers, column = NP - 1, NZ - 1
    steps, reduced = pl.pallas_call(
        main_kernel,
        out_shape=(
            jax.ShapeDtypeStruct((5, CELLS_HERE * CS), f32),
            jax.ShapeDtypeStruct((6, 32, 128), f32),
        ),
        in_specs=[SMEM, SMEM, SMEM] + [VMEM] * 6,
        out_specs=(VMEM, VMEM),
        scratch_shapes=[
            pltpu.VMEM((NC * NZ, NY * NX, 8, 128), f32),
            pltpu.SMEM((4, TR), jnp.int32),
            pltpu.VMEM((10 * TR, 128), f32),
            pltpu.VMEM((8 * TR, 128), f32),
            pltpu.VMEM((TR, 128), jnp.int32),
            pltpu.VMEM((TR, 128), jnp.int32),
            pltpu.VMEM((5 * TR, 128), f32),
            pltpu.VMEM((5, 2, DEV, 128), f32),
            pltpu.VMEM((TR * KB, 128), bf16),
            pltpu.VMEM((TR * KB, 128), bf16),
            pltpu.VMEM((4 * TR, 128), f32),
            pltpu.VMEM((TR, 128), f32),
            pltpu.VMEM((24, CELLS_HERE * CS), f32),
            pltpu.VMEM((2 * DEV, TR), bf16),
            pltpu.VMEM((QIN * KB, 2 * NP * QIN), bf16),
            pltpu.VMEM((TR, 128), f32),
            pltpu.VMEM((DEV, 128), f32),
            pltpu.VMEM((5, NP, 2, QIN, 128), f32),
            pltpu.VMEM((NP, QIN, 128), f32),
            pltpu.VMEM((6, QIN * KB, 128), f32),
            pltpu.VMEM((6, NZ * KB, 128), f32),
            pltpu.VMEM((6, NZ * KB, 128), f32),
            pltpu.VMEM((6, NZ, KB, 128), f32),
            dma((column,)), dma((column,)), dma((peers,)), dma((peers,)), dma, dma,
            dma((5, peers)), dma((5, peers)), dma((peers,)), dma((peers,)), dma((6,)), dma((6,)),
            dma((6, column)), dma((6, column)), dma((2,)), dma((2,)),
        ],
        compiler_params=pltpu.CompilerParams(collective_id=0, has_side_effects=True),
        name="exchange",
    )(
        cell_counts, owners, block_slot, attitude,
        star_partials, attitude_partials, observed, phase, knot_offset,
    )
    attitude_step, star_step = pl.pallas_call(
        sweep_kernel,
        out_shape=(
            jax.ShapeDtypeStruct((4, 256), f32),
            jax.ShapeDtypeStruct((5, CELLS_HERE * CS), f32),
        ),
        in_specs=[VMEM, VMEM],
        out_specs=(VMEM, VMEM),
        name="sweeps",
    )(reduced, steps)
    return (star_step, attitude_step)


def solution(mesh):
    both = ("cells", "tm")
    placed = (
        P(None, both), P(None, None, both), P(None, None, both), P(None, both), P(None, both), P(None, both),
        P(both), P(both, None, None), P(both, None),
    )
    return jax.shard_map(
        per_device, mesh=mesh, in_specs=placed, out_specs=(P(None, both), P(None, both)), check_vma=False
    )
```

```python
import functools

import jax
import jax.numpy as jnp
from jax import lax
from jax.experimental import pallas as pl
from jax.experimental.pallas import tpu as pltpu
from jax.sharding import PartitionSpec as P

NT, CS, KB, ITERS = 64, 128, 16, 6
NX, NY, NZ, NC = 4, 4, 8, 2
NP = NX * NY
DEV = NP * NZ * NC
QIN = NZ * NC
CELLS_HERE = 4
TR = CELLS_HERE * NT
ID_LANE = 63
EARLY = 2
MESH = pl.DeviceIdType.MESH
f32, bf16 = jnp.float32, jnp.bfloat16
PAIRS = [(m, n) for m in range(4) for n in range(m, 4)]
PAIR_OF = {pair: i for i, pair in enumerate(PAIRS)}
SHIFTS = [(t, i) for t in range(4) for i in range(4 - t)]
SHIFT_OF = {pair: i for i, pair in enumerate(SHIFTS)}
VMEM = pl.BlockSpec(memory_space=pltpu.VMEM)
SMEM = pl.BlockSpec(memory_space=pltpu.SMEM)


def place():
    cells, x = lax.axis_index("cells"), lax.axis_index("tm")
    z, y, c = lax.div(cells, NY * NC), lax.rem(lax.div(cells, NC), NY), lax.rem(cells, NC)
    return x, y, z, c


def device(x, y, z, c):
    return ((z * NY + y) * NC + c, x)


def remote(src, dst, send, recv, target):
    return pltpu.make_async_remote_copy(
        src_ref=src, dst_ref=dst, send_sem=send, recv_sem=recv, device_id=target, device_id_type=MESH
    )


def plane_peers(x, y, z, c):
    xs = [x] + [lax.rem(x + d, NX) for d in range(1, NX)]
    ys = [y] + [lax.rem(y + d, NY) for d in range(1, NY)]
    return [(i * NY + j, device(i, j, z, c)) for i in xs for j in ys][1:]


def column_peers(x, y, z, c):
    return [(zz, device(x, y, zz, c)) for zz in [lax.rem(z + i, NZ) for i in range(1, NZ)]]


def greet(targets):
    barrier = pltpu.get_barrier_semaphore()
    for target in targets:
        pl.semaphore_signal(barrier, inc=1, device_id=target, device_id_type=MESH)
    return lambda: pl.semaphore_wait(barrier, len(targets))


def split(value):
    high = value.astype(bf16)
    low = (value - high.astype(f32)).astype(bf16)
    return high, low


def cholesky(entries, size):
    lower = [[None] * size for _ in range(size)]
    inverse = [None] * size
    for col in range(size):
        total = entries(col, col)
        for k in range(col):
            total = total - lower[col][k] * lower[col][k]
        inverse[col] = 1.0 / jnp.sqrt(total)
        for row in range(col + 1, size):
            acc = entries(row, col)
            for k in range(col):
                acc = acc - lower[row][k] * lower[col][k]
            lower[row][col] = acc * inverse[col]
    return lower, inverse


def substitute(lower, inverse, rhs, size):
    forward = []
    for row in range(size):
        acc = rhs[row]
        for k in range(row):
            acc = acc - lower[row][k] * forward[k]
        forward.append(acc * inverse[row])
    answer = [None] * size
    for row in reversed(range(size)):
        acc = forward[row]
        for k in range(row + 1, size):
            acc = acc - lower[k][row] * answer[k]
        answer[row] = acc * inverse[row]
    return answer


def spline(t, live):
    square = t * t
    cube = square * t
    rest = 1.0 - t
    return [
        rest * rest * rest * (1.0 / 6.0) * live,
        (3.0 * cube - 6.0 * square + 4.0) * (1.0 / 6.0) * live,
        (-3.0 * cube + 3.0 * square + 3.0 * t + 1.0) * (1.0 / 6.0) * live,
        cube * (1.0 / 6.0) * live,
    ]


def spread(rows, hits):
    value = jnp.zeros((16, 128), f32)
    for row, hit in reversed(list(zip(rows, hits))):
        value = jnp.where(hit, jnp.broadcast_to(row, (16, 128)), value)
    return value


def nt_dot(left, right):
    return lax.dot_general(left, right, (((1,), (1,)), ((), ())), preferred_element_type=f32)


def aligned(value):
    return pl.multiple_of(value, 8)


def main_kernel(
    counts, owners, slots, att_in, star, axis, observed, phase, offset,
    step_ref, out,
    att, found, cross, parts, offs, ownm, nrm, pay, sh, sl, table, first, sums, order, pick, grads, gpay, got, ggot,
    comb, part, zsum, zgot,
    zs, zr, ps, pr, cs, cr, ns, nr, gs, gr, ws, wr, us, ur, hs, hr,
):
    x, y, z, c = place()
    plane, column = plane_peers(x, y, z, c), column_peers(x, y, z, c)
    partner = device(x, y, z, 1 - c)
    rank = ((z * NY + y) * NC + c) * NX + x
    after, before = lax.rem(rank + 1, DEV), lax.rem(rank + DEV - 1, DEV)
    right, left = [(lax.div(d, NX), lax.rem(d, NX)) for d in (after, before)]
    all_here = greet([t for _, t in plane] + [t for _, t in column] + [partner, right, left])
    here = x * NY + y
    spot = y * NX + x

    sub8 = lax.broadcasted_iota(jnp.int32, (8, 128), 0)
    lane8 = lax.broadcasted_iota(jnp.int32, (8, 128), 1)
    knot = lax.broadcasted_iota(jnp.int32, (16, 128), 0)
    att[c * NZ + z, spot, 0:4, :] = att_in[:, 0:128]
    att[c * NZ + z, spot, 4:8, :] = att_in[:, 128:256]

    for cell in range(CELLS_HERE):
        lanes = slice(cell * CS, (cell + 1) * CS)

        def prepare(g, carry, cell=cell, lanes=lanes):
            rows = pl.ds(aligned(g * 8), 8)
            at = cell * NT + g * 8
            live = jnp.where(sub8 + g * 8 < counts[cell], 1.0, 0.0)
            b = spline(phase[rows, lanes], live)
            offs[pl.ds(aligned(at), 8), :] = offset[rows, lanes]
            for n, (shift, i) in enumerate(SHIFTS):
                cross[pl.ds(aligned(n * TR + at), 8), :] = b[i] * b[i + shift]
            for m in range(4):
                parts[pl.ds(aligned(m * TR + at), 8), :] = axis[m, rows, lanes]
                parts[pl.ds(aligned((4 + m) * TR + at), 8), :] = b[m]
            return carry

        lax.fori_loop(0, NT // 8, prepare, 0)

    def sides(at):
        gap = knot - jnp.broadcast_to(offs[pl.ds(at, 1), :], (16, 128))
        hits = [gap == i for i in range(4)]
        right = jnp.concatenate(
            [
                spread([cross[pl.ds(SHIFT_OF[(s, i)] * TR + at, 1), :] for i in range(4 - s)], hits)
                for s in range(4)
            ],
            axis=0,
        )
        a = [jnp.broadcast_to(parts[pl.ds(m * TR + at, 1), :], (8, 128)) for m in range(4)]
        top = jnp.where(sub8 == 4, a[1], a[0]) * jnp.where(
            sub8 == 0, a[0], jnp.where(sub8 == 2, a[2], jnp.where(sub8 == 3, a[3], a[1]))
        )
        bottom = jnp.where(sub8 < 2, a[1], jnp.where(sub8 == 4, a[3], a[2])) * jnp.where(
            (sub8 == 0) | (sub8 == 2), a[2], a[3]
        )
        rh, rl = split(right)
        lh, ll = split(jnp.concatenate([top, bottom], axis=0))
        return jnp.concatenate([lh, ll], axis=0), jnp.concatenate([rh, rl], axis=0)

    def finish(at, slot, big):
        total = big[0:16] + big[16:32]
        total = total + pltpu.roll(total, 64, 1)
        packed = jnp.where(lane8 < 64, total[0:8], total[8:16])
        packed = jnp.where((sub8 == 0) & (lane8 == ID_LANE), slot.astype(f32), packed)
        nrm[pl.ds(at, 5, stride=TR), :] = packed[0:5]

    blank = jnp.zeros((32, 128), bf16)

    def normals(g, carry):
        for jj in range(0, 32, 2):
            at = g * 32 + jj
            left0, right0 = sides(at)
            left1, right1 = sides(at + 1)
            left = jnp.concatenate(
                [jnp.concatenate([left0, blank], axis=1), jnp.concatenate([blank, left1], axis=1)], axis=0
            )
            big = nt_dot(left, jnp.concatenate([right0, right1], axis=1))
            for e in range(2):
                slot = slots[lax.shift_right_logical(g, 1), (g & 1) * 32 + jj + e]
                finish(at + e, slot, big[e * 32:(e + 1) * 32])
                owner = owners[lax.shift_right_logical(g, 1), (g & 1) * 32 + jj + e]
                ownm[pl.ds(at + e, 1), :] = jnp.full((1, 128), owner, jnp.int32)
                found[0, at + e] = ((owner & 4) << 1) | lax.shift_right_logical(owner, 5)
                found[1, at + e] = lax.shift_right_logical(owner & 24, 1) | (owner & 3)
                found[2, at + e] = lax.shift_right_logical(slot & 8, 1)
                found[3, at + e] = slot & 7
        return carry

    lax.fori_loop(0, 4, normals, 0)

    all_here()
    slab = att.at[c * NZ + z, spot]
    lines = att.at[pl.ds(c * NZ, NZ), spot]
    sheet = att.at[c * NZ + z]
    near = [remote(slab, slab, zs.at[i], zr.at[i], t) for i, (_, t) in enumerate(column)]
    wide = [remote(lines, lines, ps.at[i], pr.at[i], t) for i, (_, t) in enumerate(plane)]
    flat = [remote(slab, slab, ps.at[i], pr.at[i], t) for i, (_, t) in enumerate(plane)]
    deep = [remote(sheet, sheet, zs.at[i], zr.at[i], t) for i, (_, t) in enumerate(column)]

    def start_all(copies):
        for copy in copies:
            copy.start()

    def arrive(copies):
        for copy in copies:
            copy.wait_recv()

    def leave(copies):
        for copy in copies:
            copy.wait_send()

    pl.when(c == 0)(lambda: start_all(near))
    pl.when(c == 1)(lambda: start_all(flat))

    lax.fori_loop(4, 6, normals, 0)

    @pl.when(c == 1)
    def _():
        arrive(flat)
        start_all(deep)

    lax.fori_loop(6, TR // 32, normals, 0)

    owner = jnp.concatenate([ownm[...], ownm[...]], axis=1)
    other = owner.astype(f32).T
    left_of = lax.broadcasted_iota(jnp.int32, (TR, TR), 1) < lax.broadcasted_iota(jnp.int32, (TR, TR), 0)
    same = jnp.where((owner.astype(f32) == other) & left_of, 1.0, 0.0)
    place_in = jnp.sum(same, axis=1, keepdims=True).astype(jnp.int32)
    q = ((owner & 3) << 6) | ((owner & 24) << 1) | ((owner & 4) << 1) | lax.shift_right_logical(owner, 5)
    code = q + place_in * DEV
    target = lax.broadcasted_iota(jnp.int32, (TR, DEV), 1)
    for s in range(2):
        order[s * DEV:(s + 1) * DEV, :] = jnp.where(code == target + s * DEV, 1.0, 0.0).T.astype(bf16)

    @pl.when(c == 0)
    def _():
        arrive(near)
        start_all(wide)

    def doubled(matrix, data):
        big = jnp.dot(matrix, jnp.concatenate(split(data), axis=1), preferred_element_type=f32)
        return big[:, 0:128] + big[:, 128:256]

    terms = []
    for r in range(5):
        sorted_rows = doubled(order[...], nrm[r * TR:(r + 1) * TR, :])
        for s in range(2):
            pay[r, s] = sorted_rows[s * DEV:(s + 1) * DEV]
        terms.append([
            remote(pay.at[r, :, pl.ds(p * QIN, QIN), :], got.at[r, here], ns.at[r, i], nr.at[r, i], t)
            for i, (p, t) in enumerate(plane)
        ])
        if r < EARLY:
            start_all(terms[r])
    got[:, here] = pay[:, :, pl.ds(pl.multiple_of(here * QIN, QIN), QIN), :]

    def spreads(g, carry):
        pieces = []
        for jj in range(8):
            at = g * 8 + jj
            gap = knot - jnp.broadcast_to(offs[pl.ds(at, 1), :], (16, 128))
            pieces.append(spread([parts[pl.ds((4 + i) * TR + at, 1), :] for i in range(4)], [gap == i for i in range(4)]))
        high, low = split(jnp.concatenate(pieces, axis=0))
        where = pl.ds(pl.multiple_of(g * 128, 128), 128)
        sh[where, :] = high
        sl[where, :] = low
        return carry

    lax.fori_loop(0, TR // 8, spreads, 0)

    for cell in range(CELLS_HERE):
        lanes = slice(cell * CS, (cell + 1) * CS)

        def squares(g, acc, cell=cell, lanes=lanes):
            rows = pl.ds(aligned(g * 8), 8)
            live = jnp.where(sub8 + g * 8 < counts[cell], 1.0, 0.0)
            p = [star[m, rows, lanes] * live for m in range(5)]
            both = [p[i] * p[j] for i in range(5) for j in range(i + 1)]
            return tuple(s + term for s, term in zip(acc, both))

        acc = lax.fori_loop(0, NT // 8, squares, tuple(jnp.zeros((8, 128), f32) for _ in range(15)))
        for n in range(15):
            sums[n:n + 1, lanes] = jnp.sum(acc[n], axis=0, keepdims=True)

    def entry(i, j):
        n = i * (i + 1) // 2 + j
        return sums[n:n + 1, :] + (1.0 if i == j else 0.0)

    lower, inverse = cholesky(entry, 5)

    pl.when(c == 0)(lambda: arrive(wide))
    pl.when(c == 1)(lambda: arrive(deep))
    whole = att.at[pl.ds(c * NZ, NZ)]
    gather_c = remote(whole, whole, cs, cr, partner)
    gather_c.start()
    for r in range(EARLY, 5):
        start_all(terms[r])
    gather_c.wait_recv()

    lane4 = lax.broadcasted_iota(jnp.int32, (4, 128), 1) // KB

    def choose(g, carry):
        for jj in range(8):
            at = g * 8 + jj
            rows4 = att[found[0, at], found[1, at], pl.ds(found[2, at], 4), :]
            table[pl.ds(g * 32 + jj, 4, stride=8), :] = jnp.where(lane4 == found[3, at], rows4, 0.0)
        return carry

    lax.fori_loop(0, TR // 8, choose, 0)

    lane32 = lax.broadcasted_iota(jnp.int32, (32, 128), 1)
    row32 = lax.broadcasted_iota(jnp.int32, (32, 128), 0)
    own = (lane32 // KB) == (row32 % 8)

    def fold(value):
        for shift in (64, 32, 16):
            value = value + pltpu.roll(value, shift, 1)
        return value

    for cell in range(CELLS_HERE):
        lanes = slice(cell * CS, (cell + 1) * CS)

        def predict(g, acc, cell=cell, lanes=lanes):
            rows = pl.ds(aligned(g * 8), 8)
            gg = cell * 8 + g
            live = jnp.where(sub8 + g * 8 < counts[cell], 1.0, 0.0)
            coeff = jnp.where(own, fold(table[pl.ds(aligned(gg * 32), 32), :]), 0.0)
            high, low = split(coeff)
            where = pl.ds(pl.multiple_of(gg * 128, 128), 128)
            big = jnp.dot(jnp.concatenate([high, low], axis=0), sh[where, :], preferred_element_type=f32)
            fit = big[0:32] + big[32:64] + jnp.dot(high, sl[where, :], preferred_element_type=f32)
            value = live * observed[rows, lanes]
            for m in range(4):
                value = value - axis[m, rows, lanes] * fit[m * 8:(m + 1) * 8]
            first[pl.ds(aligned(gg * 8), 8), :] = value
            return tuple(s + star[n, rows, lanes] * value for n, s in enumerate(acc))

        acc = lax.fori_loop(0, NT // 8, predict, tuple(jnp.zeros((8, 128), f32) for _ in range(5)), unroll=8)
        for n in range(5):
            sums[15 + n:16 + n, lanes] = jnp.sum(acc[n], axis=0, keepdims=True)

    steps = substitute(lower, inverse, [sums[15 + n:16 + n, :] for n in range(5)], 5)
    for n in range(5):
        step_ref[n:n + 1, :] = steps[n]

    for cell in range(CELLS_HERE):
        lanes = slice(cell * CS, (cell + 1) * CS)

        def gradients(g, carry, cell=cell, lanes=lanes):
            rows = pl.ds(aligned(g * 8), 8)
            gg = cell * 8 + g
            live = jnp.where(sub8 + g * 8 < counts[cell], 1.0, 0.0)
            fitted = star[0, rows, lanes] * step_ref[0:1, lanes]
            for n in range(1, 5):
                fitted = fitted + star[n, rows, lanes] * step_ref[n:n + 1, lanes]
            second = first[pl.ds(aligned(gg * 8), 8), :] - live * fitted
            high, low = split(jnp.concatenate([axis[m, rows, lanes] * second for m in range(4)], axis=0))
            where = pl.ds(pl.multiple_of(gg * 128, 128), 128)
            big = nt_dot(jnp.concatenate([high, low], axis=0), sh[where, :])
            total = big[0:32] + big[32:64] + nt_dot(high, sl[where, :])
            total = fold(jnp.where(own, total, 0.0))
            grad = jnp.zeros((8, 128), f32)
            for m in range(4):
                grad = jnp.where((lane8 // KB) % 4 == m, total[m * 8:(m + 1) * 8], grad)
            grads[pl.ds(aligned(gg * 8), 8), :] = grad
            return carry

        lax.fori_loop(0, NT // 8, gradients, 0, unroll=8)

    lane = lax.broadcasted_iota(jnp.int32, (TR, 128), 1)
    placed = doubled(order[...], grads[...])
    gpay[...] = jnp.where(lane < 64, placed[0:DEV], placed[DEV:2 * DEV])
    gterms = [
        remote(gpay.at[pl.ds(p * QIN, QIN), :], ggot.at[here], gs.at[i], gr.at[i], t) for i, (p, t) in enumerate(plane)
    ]
    for copy in gterms:
        copy.start()
    ggot[here] = gpay[pl.ds(pl.multiple_of(here * QIN, QIN), QIN), :]

    rows = NP * QIN
    cols = QIN * KB
    half = NZ * KB
    keep = pl.ds(pl.multiple_of(c * half, half), half)
    give = pl.ds(pl.multiple_of((1 - c) * half, half), half)
    swaps = [remote(comb.at[r, give, :], part.at[r], ws.at[r], wr.at[r], partner) for r in range(6)]
    along = [
        [
            remote(zsum.at[r, pl.ds(zz * KB, KB), :], zgot.at[r, z], us.at[r, i], ur.at[r, i], t)
            for i, (zz, t) in enumerate(column)
        ]
        for r in range(6)
    ]

    def forward(r):
        swaps[r].wait_recv()
        zsum[r] = comb[r, keep, :] + part[r]
        for copy in along[r]:
            copy.start()
        zgot[r, z] = zsum[r, pl.ds(pl.multiple_of(z * KB, KB), KB), :]

    for r in range(6):
        for copy in terms[r] if r < 5 else gterms:
            copy.wait_recv()
        if r == 0:
            row = lax.broadcasted_iota(jnp.int32, (rows, cols), 0)
            col = lax.broadcasted_iota(jnp.int32, (rows, cols), 1)
            local = (col - (row % QIN) * KB).astype(f32)
            for s in range(2):
                ids = got[0, :, s, :, :].reshape(rows, 128)[:, ID_LANE:ID_LANE + 1]
                pick[:, s * rows:(s + 1) * rows] = jnp.where(local == ids, 1.0, 0.0).T.astype(bf16)
        if r < 5:
            data = jnp.concatenate([got[r, :, s, :, :].reshape(rows, 128) for s in range(2)], axis=0)
        else:
            both = ggot[...].reshape(rows, 128)
            data = jnp.concatenate([jnp.where(lane < 64, both, 0.0), jnp.where(lane < 64, 0.0, both)], axis=0)
        comb[r] = doubled(pick[...], data)
        swaps[r].start()
        if r > 0:
            forward(r - 1)
    forward(5)
    for group in along:
        for copy in group:
            copy.wait_recv()
    for r in range(6):
        total = zgot[r, 0]
        for i in range(1, NZ):
            total = total + zgot[r, i]
        out[r, 8:24, :] = total
    halo = [
        remote(out.at[:, 16:24, :], out.at[:, 0:8, :], hs.at[0], hr.at[0], right),
        remote(out.at[:, 8:16, :], out.at[:, 24:32, :], hs.at[1], hr.at[1], left),
    ]
    for copy in halo:
        copy.start()
    pl.when(c == 0)(lambda: leave(near + wide))
    pl.when(c == 1)(lambda: leave(flat + deep))
    leave([gather_c] + sum(terms, []) + gterms + swaps + sum(along, []))
    for copy in halo:
        copy.wait()


def sweep_kernel(red, steps, out, steps_out):
    steps_out[...] = steps[...]
    rank = lax.axis_index("cells") * NX + lax.axis_index("tm")
    shape = (24, 128)
    row = lax.broadcasted_iota(jnp.int32, shape, 0)
    lane = lax.broadcasted_iota(jnp.int32, shape, 1)
    k = lane % KB
    beyond = ((row == 23) & (rank == 0)) | ((row == 16) & (rank == DEV - 1))
    valid = jnp.where(beyond, 0.0, 1.0)
    last = lax.broadcasted_iota(jnp.int32, (8, 128), 0) == 7

    def loaded(r):
        return jnp.concatenate([red[r, 8:24], jnp.where(last, red[r, 0:8], red[r, 24:32])], axis=0)

    comps = [loaded(r) for r in range(6)]
    ahead, behind = {}, {}
    for n in range(10):
        comp = comps[n % 5]
        start = (n // 5) * 64
        for t in range(4):
            value = jnp.take_along_axis(comp, start + t * 16 + k, axis=1)
            ahead[n, t] = jnp.where(k + t < KB, value, 0.0) if t else value
            if t:
                value = jnp.take_along_axis(comp, start + t * 16 + (k + KB - t) % KB, axis=1)
                behind[n, t] = jnp.where(k >= t, value, 0.0)
    for n, (i, j) in enumerate(PAIRS):
        if i == j:
            ahead[n, 0] = ahead[n, 0] + 34.0
    fold = comps[5]
    fold = fold + pltpu.roll(fold, 64, 1)
    gradient = [jnp.take_along_axis(fold, m * KB + k, axis=1) for m in range(4)]

    def pair(i, j):
        return PAIR_OF[(min(i, j), max(i, j))]

    lower, inverse = cholesky(lambda i, j: ahead[pair(i, j), 0], 4)
    x = [0.5 * v * valid for v in substitute(lower, inverse, gradient, 4)]
    for _ in range(ITERS - 1):
        misfit = list(gradient)
        for n in range(4):
            up = {t: pltpu.roll(x[n], 128 - t, 1) for t in (1, 2, 3)}
            down = {t: pltpu.roll(x[n], t, 1) for t in (1, 2, 3)}
            for m in range(4):
                p = pair(m, n)
                acc = ahead[p, 0] * x[n]
                for t in (1, 2, 3):
                    acc = acc + ahead[p, t] * up[t] + behind[p, t] * down[t]
                misfit[m] = misfit[m] - acc
            before = jnp.where(k == 0, pltpu.roll(down[1], 1, 0), down[1])
            after = jnp.where(k == KB - 1, pltpu.roll(up[1], 23, 0), up[1])
            misfit[n] = misfit[n] + 16.0 * (before + after)
        x = [(v + 0.5 * w) * valid for v, w in zip(x, substitute(lower, inverse, misfit, 4))]
    sub8 = lax.broadcasted_iota(jnp.int32, (8, 128), 0)
    keep = sub8 == lax.broadcasted_iota(jnp.int32, (8, 128), 1) // KB
    for m in range(4):
        for h in range(2):
            part = jnp.where(keep, x[m][h * 8:8 + h * 8], 0.0)
            out[m:m + 1, h * 128:(h + 1) * 128] = jnp.sum(part, axis=0, keepdims=True)


def per_device(
    attitude, star_partials, attitude_partials, observed, phase, knot_offset, cell_counts, interval_owner, block_slot
):
    dma = pltpu.SemaphoreType.DMA
    owners = interval_owner.reshape(CELLS_HERE, NT)
    peers, column = NP - 1, NZ - 1
    steps, reduced = pl.pallas_call(
        main_kernel,
        out_shape=(
            jax.ShapeDtypeStruct((5, CELLS_HERE * CS), f32),
            jax.ShapeDtypeStruct((6, 32, 128), f32),
        ),
        in_specs=[SMEM, SMEM, SMEM] + [VMEM] * 6,
        out_specs=(VMEM, VMEM),
        scratch_shapes=[
            pltpu.VMEM((NC * NZ, NY * NX, 8, 128), f32),
            pltpu.SMEM((4, TR), jnp.int32),
            pltpu.VMEM((10 * TR, 128), f32),
            pltpu.VMEM((8 * TR, 128), f32),
            pltpu.VMEM((TR, 128), jnp.int32),
            pltpu.VMEM((TR, 128), jnp.int32),
            pltpu.VMEM((5 * TR, 128), f32),
            pltpu.VMEM((5, 2, DEV, 128), f32),
            pltpu.VMEM((TR * KB, 128), bf16),
            pltpu.VMEM((TR * KB, 128), bf16),
            pltpu.VMEM((4 * TR, 128), f32),
            pltpu.VMEM((TR, 128), f32),
            pltpu.VMEM((24, CELLS_HERE * CS), f32),
            pltpu.VMEM((2 * DEV, TR), bf16),
            pltpu.VMEM((QIN * KB, 2 * NP * QIN), bf16),
            pltpu.VMEM((TR, 128), f32),
            pltpu.VMEM((DEV, 128), f32),
            pltpu.VMEM((5, NP, 2, QIN, 128), f32),
            pltpu.VMEM((NP, QIN, 128), f32),
            pltpu.VMEM((6, QIN * KB, 128), f32),
            pltpu.VMEM((6, NZ * KB, 128), f32),
            pltpu.VMEM((6, NZ * KB, 128), f32),
            pltpu.VMEM((6, NZ, KB, 128), f32),
            dma((column,)), dma((column,)), dma((peers,)), dma((peers,)), dma, dma,
            dma((5, peers)), dma((5, peers)), dma((peers,)), dma((peers,)), dma((6,)), dma((6,)),
            dma((6, column)), dma((6, column)), dma((2,)), dma((2,)),
        ],
        compiler_params=pltpu.CompilerParams(collective_id=0, has_side_effects=True),
        name="exchange",
    )(
        cell_counts, owners, block_slot, attitude,
        star_partials, attitude_partials, observed, phase, knot_offset,
    )
    attitude_step, star_step = pl.pallas_call(
        sweep_kernel,
        out_shape=(
            jax.ShapeDtypeStruct((4, 256), f32),
            jax.ShapeDtypeStruct((5, CELLS_HERE * CS), f32),
        ),
        in_specs=[VMEM, VMEM],
        out_specs=(VMEM, VMEM),
        name="sweeps",
    )(reduced, steps)
    return (star_step, attitude_step)


def solution(mesh):
    both = ("cells", "tm")
    placed = (
        P(None, both), P(None, None, both), P(None, None, both), P(None, both), P(None, both), P(None, both),
        P(both), P(both, None, None), P(both, None),
    )
    return jax.shard_map(
        per_device, mesh=mesh, in_specs=placed, out_specs=(P(None, both), P(None, both)), check_vma=False
    )
```
